256 devices in a mesh: row: 8 (over x, core), col: 4 (over z_lo), tp: 8 (over y, z_hi).
Axes of the slice: x: 4, y: 4, z: 8 (z_hi: 2, z_lo: 4; z = z_hi * 4 + z_lo), core: 2. Of those that a mesh axis runs over, the one named last changes fastest.
Arguments:
- tokens: bfloat16 [16384, 1024], P(('row', 'col'), 'tp'), may hold values from -6 to 6
- norm_before: bfloat16 [2, 1024], replicated, may hold values from 0.099609375 to 1.8984375
- query_weight: bfloat16 [2, 1024, 1024], P(None, None, 'tp'), may hold values from -0.1875 to 0.1875
- key_weight: bfloat16 [2, 1024, 1024], P(None, None, 'tp'), may hold values from -8 to 8
- value_weight: bfloat16 [2, 1024, 1024], P(None, None, 'tp'), may hold values from -0.1875 to 0.1875
- output_weight: bfloat16 [2, 1024, 1024], P(None, 'tp'), may hold values from -0.375 to 0.375
- norm_after: bfloat16 [2, 1024], replicated, may hold values from 0.099609375 to 1.8984375
- gate_weight: bfloat16 [2, 1024, 4096], P(None, None, 'tp'), may hold values from -0.1875 to 0.1875
- up_weight: bfloat16 [2, 1024, 4096], P(None, None, 'tp'), may hold values from -0.1875 to 0.1875
- down_weight: bfloat16 [2, 4096, 1024], P(None, 'tp'), may hold values from -0.09375 to 0.09375
- block_image: int32 [128], replicated, may hold values from 0 to 7, never falling along the last dimension, each value on 1 to 29 neighbouring positions
- image_width: int32 [8], replicated, may hold values from 16 to 64
Outputs:
- encoded: float32 [16384, 1024], P(('row', 'col'), 'tp')
The draws below stay inside these ranges and needn't reach their ends.
Inputs may be any that keep to these rules, and one draw needn't show every extreme that they name: `block_image`: image numbers never fall from block to block; each image fills 1 to 29 whole blocks of 128 patch slots, and one image fills exactly 29.
All inputs are finite; a program needn't handle non-finite values.
Results may differ from the reference program's by a relative error of at most 0.035.
The reference program's roundings to bfloat16 on the way count: a program that leaves them out, or rounds other values in their place, can miss the bound.
Values may be sent and summed in bfloat16 or wider, within the bound.
A program may use at most 64 MiB of HBM per device.

```python
import math
import jax
import jax.numpy as jnp
import numpy as np
from jax import lax

D = 1024
HEADS = 16
FF = 4096
HEAD_DIM = 64
BLK = 128
LAYERS = 2
BLOCKS = 128
TOKENS = 16384
IMAGES = 8
MOST_BLK = 29


def draw_tokens(key, part):
    base = jnp.clip(jax.random.normal(jax.random.fold_in(key, 11), (TOKENS, D), jnp.float32), -6.0, 6.0)
    return base.astype(jnp.bfloat16)


def draw_key_weight(key, part):
    base = jnp.clip(jax.random.normal(jax.random.fold_in(key, 21), (LAYERS, D, D), jnp.float32), -4.0, 4.0) * D ** (-0.5)
    return base.astype(jnp.bfloat16)


def plant(values, stream_key, low, top_value):
    shape = values.shape
    index_at = [jax.random.randint(jax.random.fold_in(stream_key, axis), (), 0, shape[axis]) for axis in range(len(shape))]
    values = values.at[tuple(index_at)].set(low)
    longest = shape.index(max(shape))
    index_at[longest] = (index_at[longest] + 1) % shape[longest]
    return values.at[tuple(index_at)].set(top_value)


def level_of(rng, extent, cuts, low, high):
    def one(position, shards_of):
        steps = jax.random.uniform(jax.random.fold_in(jax.random.fold_in(rng, 6), position), (shards_of,), jnp.float32, low / len(cuts), high / len(cuts))
        return jnp.repeat(jnp.exp(steps), extent[position] // shards_of).reshape((-1,) + (1,) * (len(extent) - position - 1))

    level = one(*cuts[0])
    for cut in cuts[1:]:
        level = level * one(*cut)
    return level


def split_up(amount, total, most, lean):
    loads = [(1 << 20) // math.isqrt(standing ** lean) + 1 for standing in range(2, amount + 1)]
    surplus, holding = total - most - (amount - 1), [1] * (amount - 1)
    while surplus > 0:
        movable = [i for i in range(amount - 1) if holding[i] < most]
        whole, budget = sum([loads[i] for i in movable]), surplus
        for i in movable:
            extra = min(most - holding[i], max(1, budget * loads[i] // whole), surplus)
            holding[i] = holding[i] + extra
            surplus = surplus - extra
    return np.array([most] + holding)


def uneven_parts(rng, amount, total, limit, slope):
    if amount == 2:
        one = jax.random.randint(rng, (), max(1, total - limit), min(limit, total - 1) + 1)
        return jnp.stack([one, total - one])
    tallies = jnp.asarray(split_up(amount, total, limit, slope), jnp.int32)
    twos = (amount - 1) // 2
    source_of, taker = tallies[1:1 + 2 * twos:2], tallies[2:2 + 2 * twos:2]
    room = jnp.minimum(source_of - 1, limit - taker)
    moved = jax.random.randint(jax.random.fold_in(rng, 1), (twos,), 0, 1 << 20) % (room + 1)
    tallies = tallies.at[1:1 + 2 * twos:2].set(source_of - moved).at[2:2 + 2 * twos:2].set(taker + moved)
    return tallies[jax.random.permutation(jax.random.fold_in(rng, 2), amount)]


def centred(stream_key, shape, scale, reach, shards=(), held_as=jnp.bfloat16):
    array = jax.random.normal(stream_key, shape, jnp.float32) * scale
    if len(shards) > 0:
        array = level_of(stream_key, shape, shards, -0.22, 0.18) * array
    return jnp.clip(array, min=-reach, max=reach).astype(held_as)


def setup_inputs(seed: int = 0) -> dict:
    key_list = jax.random.split(jax.random.key(seed), 13)
    tokens = draw_tokens(jax.random.fold_in(key_list[12], 71), 0)
    norm_before = jnp.clip(1.0 + 0.18 * jax.random.normal(key_list[1], (LAYERS, D), jnp.float32), 0.099609375, 1.8984375).astype(jnp.bfloat16)
    query_weight = centred(key_list[2], (LAYERS, D, D), D ** -0.5, 0.1875, ((2, 8),))
    key_weight = draw_key_weight(jax.random.fold_in(key_list[12], 71), 0)
    value_weight = centred(key_list[4], (LAYERS, D, D), D ** -0.5, 0.1875, ((2, 8),))
    output_weight = centred(key_list[5], (LAYERS, D, D), (4 * HEAD_DIM) ** -0.5, 0.375, ((1, 8),))
    norm_after = jnp.clip(1.0 + 0.18 * jax.random.normal(key_list[6], (LAYERS, D), jnp.float32), 0.099609375, 1.8984375).astype(jnp.bfloat16)
    gate_weight = centred(key_list[7], (LAYERS, D, FF), D ** -0.5, 0.1875, ((2, 8),))
    up_weight = centred(key_list[8], (LAYERS, D, FF), D ** -0.5, 0.1875, ((2, 8),))
    down_weight = centred(key_list[9], (LAYERS, FF, D), FF ** -0.5, 0.09375, ((1, 8),))
    block_image = jnp.searchsorted(jnp.cumsum(uneven_parts(key_list[10], IMAGES, BLOCKS, MOST_BLK, 2)), jnp.arange(BLOCKS), side="right").astype(jnp.int32)
    image_width = plant(jax.random.randint(key_list[11], (IMAGES,), BLK // 8, BLK // 2 + 1), jax.random.fold_in(key_list[11], 1), BLK // 8, (BLK // 2 + 1) - 1).astype(jnp.int32)
    return dict(tokens=tokens, norm_before=norm_before, query_weight=query_weight, key_weight=key_weight, value_weight=value_weight, output_weight=output_weight, norm_after=norm_after, gate_weight=gate_weight, up_weight=up_weight, down_weight=down_weight, block_image=block_image, image_width=image_width)


epsilon = 1e-05
theta = 10000.0
masked = -1e+30

def block_tables(block_image, image_width):
    block_total = block_image.shape[0]
    images = jnp.arange(image_width.shape[0], dtype=jnp.int32)
    member = (block_image[:, None] == images[None, :]).astype(jnp.int32)
    count = lax.optimization_barrier(jnp.sum(member, axis=0))
    start = lax.optimization_barrier(jnp.sum((block_image[:, None] < images[None, :]).astype(jnp.int32), axis=0))
    slots = count * BLK
    width = image_width.astype(jnp.int32)
    filled = slots // width * width
    first = lax.optimization_barrier(jnp.sum(member * start[None, :], axis=1))
    offset = (jnp.arange(block_total, dtype=jnp.int32) - first) * BLK
    return (block_image, offset, lax.optimization_barrier(jnp.sum(member * width[None, :], axis=1)), lax.optimization_barrier(jnp.sum(member * filled[None, :], axis=1)))

def token_rows(tables, first_block, shard_blocks):
    image, offset, width, filled = [jnp.repeat(lax.dynamic_slice_in_dim(table, first_block, shard_blocks), BLK) for table in tables]
    slot = offset + jnp.arange(shard_blocks * BLK, dtype=jnp.int32) % BLK
    return (image, slot // width, slot % width, slot < filled)

def rope_tables(patch_row, patch_column):
    half = HEAD_DIM // 2
    frequency = theta ** (-2.0 * jnp.arange(half, dtype=jnp.float32) / HEAD_DIM)
    angle = jnp.concatenate([patch_row.astype(jnp.float32)[:, None] * frequency[None, 0::2], patch_column.astype(jnp.float32)[:, None] * frequency[None, 1::2]], axis=1)
    return (jnp.cos(angle), jnp.sin(angle))

def rotate(heads, cosine, sine):
    half = heads.shape[-1] // 2
    front = heads[..., :half]
    back = heads[..., half:]
    cosine = cosine[:, None, :]
    sine = sine[:, None, :]
    return jnp.concatenate([front * cosine - back * sine, back * cosine + front * sine], axis=-1)

def normalize(values, gain):
    wide = values.astype(jnp.float32)
    scale = lax.rsqrt(lax.optimization_barrier(jnp.mean(wide * wide, axis=-1, keepdims=True)) + epsilon)
    return (wide * scale * gain.astype(jnp.float32)).astype(jnp.bfloat16)

def attention(query, keys, values, image, tags):
    rows = query.shape[0]
    block = math.gcd(rows, 256)
    margin = MOST_BLK * BLK
    length = min(rows, block + 2 * margin)
    scale = HEAD_DIM ** (-0.5)

    def one_block(index):
        begin = index * block
        key_start = jnp.clip(begin - margin, 0, rows - length)
        part_query = lax.dynamic_slice_in_dim(query, begin, block, 0).astype(jnp.float32)
        part_keys = lax.dynamic_slice_in_dim(keys, key_start, length, 0).astype(jnp.float32)
        part_values = lax.dynamic_slice_in_dim(values, key_start, length, 0).astype(jnp.float32)
        part_image = lax.dynamic_slice_in_dim(image, begin, block, 0)
        part_tags = lax.dynamic_slice_in_dim(tags, key_start, length, 0)
        scores = jnp.einsum('thd,uhd->thu', part_query, part_keys, precision=lax.Precision.HIGHEST) * scale
        allowed = (part_image[:, None] == part_tags[None, :])[:, None, :]
        top = lax.optimization_barrier(jnp.max(jnp.where(allowed, scores, masked), axis=-1, keepdims=True))
        raised = jnp.where(allowed, jnp.exp(scores - top), 0.0)
        total = lax.optimization_barrier(jnp.sum(raised, axis=-1))
        weights = lax.optimization_barrier(raised.astype(jnp.bfloat16)).astype(jnp.float32)
        summed = jnp.einsum('thu,uhd->thd', weights, part_values, precision=lax.Precision.HIGHEST)
        return (summed / total[..., None]).astype(jnp.bfloat16).reshape(block, -1)
    pieces = lax.map(one_block, jnp.arange(rows // block, dtype=jnp.int32))
    return pieces.reshape(rows, -1)

def reference(tokens, norm_before, query_weight, key_weight, value_weight, output_weight, norm_after, gate_weight, up_weight, down_weight, block_image, image_width):
    tables = block_tables(block_image, image_width)
    image, patch_row, patch_column, live = token_rows(tables, 0, block_image.shape[0])
    tags = jnp.where(live, image, -1)
    cosine, sine = rope_tables(patch_row, patch_column)
    rows = tokens.shape[0]
    hidden_state = tokens.astype(jnp.float32)
    for layer in range(LAYERS):
        normed = normalize(hidden_state, norm_before[layer])
        query = rotate(jnp.dot(normed, query_weight[layer], preferred_element_type=jnp.float32).reshape(rows, HEADS, HEAD_DIM), cosine, sine)
        query = lax.optimization_barrier(query.astype(jnp.bfloat16))
        keys = rotate(jnp.dot(normed, key_weight[layer], preferred_element_type=jnp.float32).reshape(rows, HEADS, HEAD_DIM), cosine, sine)
        keys = lax.optimization_barrier(keys.astype(jnp.bfloat16))
        values = jnp.dot(normed, value_weight[layer], preferred_element_type=jnp.float32).astype(jnp.bfloat16)
        values = lax.optimization_barrier(values).reshape(rows, HEADS, HEAD_DIM)
        attended = attention(query, keys, values, image, tags)
        middle = hidden_state + jnp.dot(attended, output_weight[layer], preferred_element_type=jnp.float32)
        post = normalize(middle, norm_after[layer])
        gate = jnp.dot(post, gate_weight[layer], preferred_element_type=jnp.float32)
        up = jnp.dot(post, up_weight[layer], preferred_element_type=jnp.float32)
        hidden = (jax.nn.silu(gate) * up).astype(jnp.bfloat16)
        hidden_state = middle + jnp.dot(hidden, down_weight[layer], preferred_element_type=jnp.float32)
    return hidden_state
```

```python
import functools

import jax
import jax.numpy as jnp
from jax import lax
from jax.experimental import pallas as pl
from jax.experimental.pallas import tpu as pltpu
from jax.sharding import PartitionSpec as P

HEAD_DIM = 64
BLK = 128
WINDOW = 30
CHUNK = 256

epsilon = 1e-05
theta = 10000.0
masked = -1e30
MESH = pl.DeviceIdType.MESH

AG, RS_Y, RS_Z, KV_Z, KV_FULL, KV_PART, KV_CORE, SEMS = 0, 16, 22, 24, 28, 32, 36, 44


def block_tables(block_image, image_width):
    block_total = block_image.shape[0]
    images = jnp.arange(image_width.shape[0], dtype=jnp.int32)
    member = (block_image[:, None] == images[None, :]).astype(jnp.int32)
    count = jnp.sum(member, axis=0)
    start = jnp.sum((block_image[:, None] < images[None, :]).astype(jnp.int32), axis=0)
    slots = count * BLK
    filled = slots // image_width * image_width
    first = jnp.sum(member * start[None, :], axis=1)
    return (
        first,
        jnp.sum(member * image_width[None, :], axis=1),
        jnp.sum(member * filled[None, :], axis=1),
    )


def rope_tables(first, width, first_block, shard_blocks):
    half = HEAD_DIM // 2
    offset = (first_block + jnp.arange(shard_blocks, dtype=jnp.int32) - first) * BLK
    slot = jnp.repeat(offset, BLK) + jnp.arange(shard_blocks * BLK, dtype=jnp.int32) % BLK
    width = jnp.repeat(width, BLK)
    frequency = theta ** (-2.0 * jnp.arange(half, dtype=jnp.float32) / HEAD_DIM)
    angle = jnp.concatenate(
        [
            (slot // width).astype(jnp.float32)[:, None] * frequency[None, 0::2],
            (slot % width).astype(jnp.float32)[:, None] * frequency[None, 1::2],
        ],
        axis=1,
    )
    cosine, sine = jnp.cos(angle), jnp.sin(angle)
    return (
        jnp.concatenate([cosine] * 4, axis=1),
        jnp.concatenate([-sine, sine, -sine, sine], axis=1),
    )


def normalize(values, gain):
    scale = lax.rsqrt(jnp.mean(values * values, axis=-1, keepdims=True) + epsilon)
    return (values * scale * gain).astype(jnp.bfloat16)


def rotate(heads, cosine, sine):
    lane = lax.broadcasted_iota(jnp.int32, heads.shape, 1)
    front = lax.rem(lane, HEAD_DIM) < HEAD_DIM // 2
    width = heads.shape[1]
    other = jnp.where(
        front,
        pltpu.roll(heads, width - HEAD_DIM // 2, 1),
        pltpu.roll(heads, HEAD_DIM // 2, 1),
    )
    return heads * cosine + other * sine


def layers_kernel(
    layers,
    window_ref,
    tokens_ref,
    cosine_ref,
    sine_ref,
    gain_before_ref,
    gain_after_ref,
    wq_hbm,
    wk_hbm,
    wv_hbm,
    wo_hbm,
    wg_hbm,
    wu_hbm,
    wd_hbm,
    out_ref,
    wq,
    wk,
    wv,
    wo,
    wg,
    wu,
    wd,
    whole,
    kv_first,
    kv_second,
    query,
    scores,
    attended,
    parts,
    parts_in,
    half_out,
    half_in,
    stream,
    weight_sem,
    send_sem,
    recv_sem,
):
    rows = tokens_ref.shape[0]
    blocks = rows // BLK
    row, col, tp = lax.axis_index("row"), lax.axis_index("col"), lax.axis_index("tp")
    high, low = tp // 2, tp % 2
    chip, core = row // 2, row % 2

    def at_tp(step):
        return (row, col, (high + step) % 4 * 2 + low)

    z_partner = (row, col, high * 2 + 1 - low)
    core_partner = (chip * 2 + 1 - core, col, tp)
    x_up = ((row + 2) % 8, col, tp)
    x_down = ((row + 6) % 8, col, tp)

    def at_col(step):
        return (row, (col + step) % 4, tp)

    weights = [
        pltpu.make_async_copy(src, dst, weight_sem.at[i])
        for i, (src, dst) in enumerate(
            zip(
                (wq_hbm, wk_hbm, wv_hbm, wo_hbm, wg_hbm, wu_hbm, wd_hbm),
                (wq, wk, wv, wo, wg, wu, wd),
                strict=True,
            )
        )
    ]
    for copy in weights:
        copy.start()

    barrier = pltpu.get_barrier_semaphore()
    peers = [at_tp(1), at_tp(2), at_tp(3), z_partner, core_partner, x_up, x_down]
    peers += [at_col(1), at_col(2), at_col(3)]
    for peer in peers:
        pl.semaphore_signal(barrier, inc=1, device_id=peer, device_id_type=MESH)
    pl.semaphore_wait(barrier, len(peers))

    stream[...] = tokens_ref[...].astype(jnp.float32)
    for copy in weights:
        copy.wait()

    def layer_body(layer):
        def send(src, dst, sem, device):
            return pltpu.make_async_remote_copy(
                src_ref=src,
                dst_ref=dst,
                send_sem=send_sem.at[layer, sem],
                recv_sem=recv_sem.at[layer, sem],
                device_id=device,
                device_id_type=MESH,
            )

        def gather(stage):
            held = whole.at[layer, stage]
            base = AG + 8 * stage
            held[tp] = stream[...].astype(jnp.bfloat16)
            sent = [send(held.at[tp], held.at[tp], base + 3, z_partner)]
            sent += [send(held.at[tp], held.at[tp], base + d - 1, at_tp(d)) for d in (1, 3, 2)]
            for copy in sent:
                copy.start()
            other = tp + 1 - 2 * low
            sent[0].wait_recv()
            passed = [send(held.at[other], held.at[other], base + 3 + d, at_tp(d)) for d in (1, 3, 2)]
            for copy in passed:
                copy.start()
            for copy in sent[1:] + passed:
                copy.wait_recv()
            for copy in sent + passed:
                copy.wait_send()

        def scatter(stage):
            own = parts.at[layer, stage]
            arrived = parts_in.at[layer, stage]
            base = RS_Y + 3 * stage
            sent = [
                send(
                    own.at[pl.ds((high + d) % 4 * 2, 2)],
                    arrived.at[d - 1],
                    base + d - 1,
                    at_tp(d),
                )
                for d in (1, 3, 2)
            ]
            for copy in sent:
                copy.start()
            for copy in sent:
                copy.wait()

            def summed(half):
                total = own[high * 2 + half].astype(jnp.float32)
                for d in range(3):
                    total = total + arrived[d, half].astype(jnp.float32)
                return total

            half_out[layer, stage] = summed(1 - low).astype(jnp.bfloat16)
            cross = send(half_out.at[layer, stage], half_in.at[layer, stage], RS_Z + stage, z_partner)
            cross.start()
            stream[...] = stream[...] + summed(low)
            cross.wait()
            stream[...] = stream[...] + half_in[layer, stage].astype(jnp.float32)

        def whole_block(stage, at):
            return jnp.concatenate(
                [whole[layer, stage, i, at, :] for i in range(8)], axis=1
            ).astype(jnp.float32)

        held_kv = (kv_first, kv_second)[layer]

        def shard(offset, number):
            return held_kv.at[pl.ds((offset * 8 + number) * blocks, blocks)]

        gather(0)

        def project(block, unused):
            at = pl.ds(pl.multiple_of(block * BLK, BLK), BLK)
            normed = normalize(
                whole_block(0, at), gain_before_ref[layer].astype(jnp.float32)
            )
            cosine, sine = cosine_ref[at, :], sine_ref[at, :]
            turned = rotate(
                jnp.dot(normed, wq[layer], preferred_element_type=jnp.float32), cosine, sine
            ).astype(jnp.bfloat16)
            query[at, :] = turned * jnp.bfloat16(HEAD_DIM**-0.5)
            here = (8 + core * 4 + col) * blocks + block
            held_kv[here, :, 0:BLK] = rotate(
                jnp.dot(normed, wk[layer], preferred_element_type=jnp.float32), cosine, sine
            ).astype(jnp.bfloat16)
            held_kv[here, :, BLK : 2 * BLK] = jnp.dot(
                normed, wv[layer], preferred_element_type=jnp.float32
            ).astype(jnp.bfloat16)
            return unused

        lax.fori_loop(0, blocks, project, 0)

        own_number = core * 4 + col
        along = [
            send(shard(1, own_number), shard(1, own_number), KV_Z + d, at_col(d)) for d in (1, 3, 2)
        ]
        for copy in along:
            copy.start()
        full_slot = 2 - 2 * core
        part_slot = 2 * core
        started = []

        def to_full(source):
            there = ((row + 6 + 4 * core) % 8, col, tp)
            return send(
                shard(1, core * 4 + source), shard(full_slot, core * 4 + source), KV_FULL + source, there
            )

        def to_part(source):
            there = ((row + 2 + 4 * core) % 8, col, tp)
            return send(
                shard(1, core * 4 + source), shard(part_slot, core * 4 + source), KV_PART + source, there
            )

        def part_needed(source):
            return ((core == 0) & (source > col)) | ((core == 1) & (source < col))

        def to_core(slot, source, sem):
            number = core * 4 + source
            return send(shard(slot, number), shard(slot, number), KV_CORE + sem + source, core_partner)

        for d in (0, 1, 3, 2):
            source = (col + 4 - d) % 4
            if d:
                send(shard(1, own_number), shard(1, own_number), KV_Z + d, at_col(d)).wait_recv()

                @pl.when(part_needed(source))
                def _():
                    to_part(source).start()

            to_full(source).start()
            to_core(1, source, 0).start()
        for d in (0, 1, 3, 2):
            source = (col + 4 - d) % 4
            to_full(source).wait_recv()
            to_core(full_slot, source, 4).start()
        for d in (0, 1, 3, 2):
            source = (col + 4 - d) % 4
            to_full(source).wait_send()
            if d:

                @pl.when(part_needed(source))
                def _():
                    to_part(source).wait()

            to_core(1, source, 0).wait()
            to_core(full_slot, source, 4).wait()
        for copy in along:
            copy.wait_send()

        lane = lax.broadcasted_iota(jnp.int32, (BLK, BLK), 1)
        chunks = WINDOW * BLK // CHUNK
        each = CHUNK // BLK

        def keys_of(begin, chunk, lanes):
            return jnp.concatenate(
                [held_kv[begin + chunk * each + i][:, lanes : lanes + BLK] for i in range(each)], axis=0
            )

        def attend(block, unused):
            at = pl.ds(pl.multiple_of(block * BLK, BLK), BLK)
            begin = window_ref[block, 0]
            shift = window_ref[block, 1]
            filled = window_ref[block, 2]
            turned = query[at, :]
            zero = jnp.zeros_like(turned)
            stacked = jnp.concatenate(
                [jnp.where(lane < HEAD_DIM, turned, zero), jnp.where(lane < HEAD_DIM, zero, turned)],
                axis=0,
            )
            best = jnp.full((2 * BLK, BLK), masked, jnp.float32)
            for chunk in range(chunks):
                keys = keys_of(begin, chunk, 0)
                found = lax.dot_general(
                    stacked, keys, (((1,), (1,)), ((), ())), preferred_element_type=jnp.float32
                )
                slot = lax.broadcasted_iota(jnp.int32, (1, CHUNK), 1) + (shift + chunk * CHUNK)
                found = jnp.where((slot >= 0) & (slot < filled), found, masked)
                scores[:, chunk * CHUNK : (chunk + 1) * CHUNK] = found
                for part in range(CHUNK // BLK):
                    best = jnp.maximum(best, found[:, part * BLK : (part + 1) * BLK])
            top = jnp.max(best, axis=1, keepdims=True)
            total = jnp.zeros((2 * BLK, BLK), jnp.float32)
            mixed = jnp.zeros((2 * BLK, BLK), jnp.float32)
            for chunk in range(chunks):
                raised = jnp.exp(scores[:, chunk * CHUNK : (chunk + 1) * CHUNK] - top)
                for part in range(CHUNK // BLK):
                    total = total + raised[:, part * BLK : (part + 1) * BLK]
                values = keys_of(begin, chunk, BLK)
                mixed = mixed + jnp.dot(
                    raised.astype(jnp.bfloat16), values, preferred_element_type=jnp.float32
                )
            mixed = mixed / jnp.sum(total, axis=1, keepdims=True)
            attended[at, :] = jnp.where(lane < HEAD_DIM, mixed[0:BLK], mixed[BLK:]).astype(
                jnp.bfloat16
            )
            return unused

        lax.fori_loop(0, blocks, attend, 0)

        def spread(stage, at, part):
            for i in range(8):
                parts[layer, stage, i, at, :] = part[:, i * BLK : (i + 1) * BLK].astype(jnp.bfloat16)

        def project_out(block, unused):
            at = pl.ds(pl.multiple_of(block * BLK, BLK), BLK)
            spread(0, at, jnp.dot(attended[at, :], wo[layer], preferred_element_type=jnp.float32))
            return unused

        lax.fori_loop(0, blocks, project_out, 0)
        scatter(0)
        gather(1)

        def feed(block, unused):
            at = pl.ds(pl.multiple_of(block * 2 * BLK, BLK), 2 * BLK)
            post = normalize(whole_block(1, at), gain_after_ref[layer].astype(jnp.float32))
            gate = jnp.dot(post, wg[layer], preferred_element_type=jnp.float32)
            up = jnp.dot(post, wu[layer], preferred_element_type=jnp.float32)
            hidden = (gate / (1.0 + jnp.exp(-gate)) * up).astype(jnp.bfloat16)
            spread(1, at, jnp.dot(hidden, wd[layer], preferred_element_type=jnp.float32))
            return unused

        lax.fori_loop(0, blocks // 2, feed, 0)
        scatter(1)

    for layer in range(layers):
        layer_body(layer)
    out_ref[...] = stream[...]


def local(
    tokens,
    norm_before,
    query_weight,
    key_weight,
    value_weight,
    output_weight,
    norm_after,
    gate_weight,
    up_weight,
    down_weight,
    block_image,
    image_width,
):
    rows = tokens.shape[0]
    blocks = rows // BLK
    layers = query_weight.shape[0]
    place = lax.axis_index(("row", "col"))
    first, width, filled = [
        lax.dynamic_slice_in_dim(table, place * blocks, blocks)
        for table in block_tables(block_image, image_width)
    ]
    cosine, sine = rope_tables(first, width, place * blocks, blocks)
    origin = (place // 8 - 1) * 8 * blocks
    begin = jnp.minimum(first, place * blocks + 8 * blocks - WINDOW)
    window = jnp.stack([begin - origin, (begin - first) * BLK, filled], axis=1)
    hbm = pl.BlockSpec(memory_space=pl.ANY)
    vmem = pl.BlockSpec(memory_space=pltpu.VMEM)
    bf16, f32 = jnp.bfloat16, jnp.float32
    return pl.pallas_call(
        functools.partial(layers_kernel, layers),
        out_shape=jax.ShapeDtypeStruct(tokens.shape, f32),
        in_specs=[pl.BlockSpec(memory_space=pltpu.SMEM)] + [vmem] * 5 + [hbm] * 7,
        out_specs=vmem,
        scratch_shapes=[
            pltpu.VMEM(w.shape, bf16)
            for w in (
                query_weight,
                key_weight,
                value_weight,
                output_weight,
                gate_weight,
                up_weight,
                down_weight,
            )
        ]
        + [
            pltpu.VMEM((layers, 2, 8, rows, BLK), bf16),
            pltpu.VMEM((24 * blocks, BLK, 2 * BLK), bf16),
            pltpu.VMEM((24 * blocks, BLK, 2 * BLK), bf16),
            pltpu.VMEM((rows, BLK), bf16),
            pltpu.VMEM((2 * BLK, WINDOW * BLK), f32),
            pltpu.VMEM((rows, BLK), bf16),
            pltpu.VMEM((layers, 2, 8, rows, BLK), bf16),
            pltpu.VMEM((layers, 2, 3, 2, rows, BLK), bf16),
            pltpu.VMEM((layers, 2, rows, BLK), bf16),
            pltpu.VMEM((layers, 2, rows, BLK), bf16),
            pltpu.VMEM((rows, BLK), f32),
            pltpu.SemaphoreType.DMA((7,)),
            pltpu.SemaphoreType.DMA((layers, SEMS)),
            pltpu.SemaphoreType.DMA((layers, SEMS)),
        ],
        compiler_params=pltpu.CompilerParams(
            collective_id=0, has_side_effects=True, vmem_limit_bytes=56 << 20
        ),
        name="encoder_layers",
    )(
        window,
        tokens,
        cosine,
        sine,
        norm_before[:, None, :],
        norm_after[:, None, :],
        query_weight,
        key_weight,
        value_weight,
        output_weight,
        gate_weight,
        up_weight,
        down_weight,
    )


def solution(mesh):
    placed = (
        P(("row", "col"), "tp"),
        P(),
        P(None, None, "tp"),
        P(None, None, "tp"),
        P(None, None, "tp"),
        P(None, "tp", None),
        P(),
        P(None, None, "tp"),
        P(None, None, "tp"),
        P(None, "tp", None),
        P(),
        P(),
    )
    return jax.shard_map(
        local, mesh=mesh, in_specs=placed, out_specs=P(("row", "col"), "tp"), check_vma=False
    )
```

```python
import functools

import jax
import jax.numpy as jnp
from jax import lax
from jax.experimental import pallas as pl
from jax.experimental.pallas import tpu as pltpu
from jax.sharding import PartitionSpec as P

HEAD_DIM = 64
BLK = 128
WINDOW = 30
CHUNK = 256

epsilon = 1e-05
theta = 10000.0
masked = -1e30
MESH = pl.DeviceIdType.MESH

UNIT = 2

AG_X, AG_A, RS_Y, OUT_W, KV = 0, 32, 64, 80, 96
KV_UP, KV_DOWN, KV_FULL, KV_PART, KV_CORE, KV_BACK, KV_SEMS = 0, 4, 8, 12, 16, 20, 24
SEMS = KV + 2 * KV_SEMS


def block_tables(block_image, image_width):
    block_total = block_image.shape[0]
    images = jnp.arange(image_width.shape[0], dtype=jnp.int32)
    member = (block_image[:, None] == images[None, :]).astype(jnp.int32)
    count = jnp.sum(member, axis=0)
    start = jnp.sum((block_image[:, None] < images[None, :]).astype(jnp.int32), axis=0)
    slots = count * BLK
    filled = slots // image_width * image_width
    first = jnp.sum(member * start[None, :], axis=1)
    return (
        first,
        jnp.sum(member * image_width[None, :], axis=1),
        jnp.sum(member * filled[None, :], axis=1),
    )


def rope_tables(first, width, first_block, shard_blocks):
    half = HEAD_DIM // 2
    offset = (first_block + jnp.arange(shard_blocks, dtype=jnp.int32) - first) * BLK
    slot = jnp.repeat(offset, BLK) + jnp.arange(shard_blocks * BLK, dtype=jnp.int32) % BLK
    width = jnp.repeat(width, BLK)
    frequency = theta ** (-2.0 * jnp.arange(half, dtype=jnp.float32) / HEAD_DIM)
    angle = jnp.concatenate(
        [
            (slot // width).astype(jnp.float32)[:, None] * frequency[None, 0::2],
            (slot % width).astype(jnp.float32)[:, None] * frequency[None, 1::2],
        ],
        axis=1,
    )
    cosine, sine = jnp.cos(angle), jnp.sin(angle)
    return (
        jnp.concatenate([cosine] * 4, axis=1),
        jnp.concatenate([-sine, sine, -sine, sine], axis=1),
    )


def normalize(values, gain):
    scale = lax.rsqrt(jnp.mean(values * values, axis=-1, keepdims=True) + epsilon)
    return (values * scale * gain).astype(jnp.bfloat16)


def rotate(heads, cosine, sine):
    lane = lax.broadcasted_iota(jnp.int32, heads.shape, 1)
    front = lax.rem(lane, HEAD_DIM) < HEAD_DIM // 2
    width = heads.shape[1]
    other = jnp.where(
        front,
        pltpu.roll(heads, width - HEAD_DIM // 2, 1),
        pltpu.roll(heads, HEAD_DIM // 2, 1),
    )
    return heads * cosine + other * sine


def layers_kernel(
    layers,
    window_ref,
    tokens_ref,
    cosine_ref,
    sine_ref,
    gain_before_ref,
    gain_after_ref,
    wq_hbm,
    wk_hbm,
    wv_hbm,
    wo_hbm,
    wg_hbm,
    wu_hbm,
    wd_hbm,
    out_ref,
    wq,
    wk,
    wv,
    wo,
    wg,
    wu,
    wd,
    inputs,
    mixes,
    kv_first,
    kv_second,
    query,
    scores,
    head_part,
    parts,
    parts_in,
    half_out,
    half_in,
    stream,
    weight_sem,
    send_sem,
    recv_sem,
):
    rows = tokens_ref.shape[0]
    blocks = rows // BLK
    row, col, tp = lax.axis_index("row"), lax.axis_index("col"), lax.axis_index("tp")
    high, low = tp // 2, tp % 2
    chip, core = row // 2, row % 2
    other = high * 2 + 1 - low

    def at_tp(step):
        return (row, col, (high + step) % 4 * 2 + low)

    z_partner = (row, col, other)
    core_partner = (chip * 2 + 1 - core, col, tp)
    x_full = ((row + 6 + 4 * core) % 8, col, tp)
    x_part = ((row + 2 + 4 * core) % 8, col, tp)
    z_up = (row, (col + 1) % 4, tp)
    z_down = (row, (col + 3) % 4, tp)

    own_out_rows = pl.ds(pl.multiple_of(tp * BLK, BLK), BLK)
    weights = [
        pltpu.make_async_copy(src, dst, weight_sem.at[i])
        for i, (src, dst) in enumerate(
            [(wo_hbm.at[i], wo.at[i, own_out_rows]) for i in range(layers)]
            + [(wq_hbm, wq), (wk_hbm, wk), (wv_hbm, wv), (wg_hbm, wg), (wu_hbm, wu), (wd_hbm, wd)]
        )
    ]
    for copy in weights:
        copy.start()

    barrier = pltpu.get_barrier_semaphore()
    peers = [at_tp(1), at_tp(2), at_tp(3), z_partner, core_partner, x_full, x_part, z_up, z_down]
    for peer in peers:
        pl.semaphore_signal(barrier, inc=1, device_id=peer, device_id_type=MESH)
    pl.semaphore_wait(barrier, len(peers))

    pending = []

    def send(src, dst, layer, sem, device):
        return pltpu.make_async_remote_copy(
            src_ref=src,
            dst_ref=dst,
            send_sem=send_sem.at[layer, sem],
            recv_sem=recv_sem.at[layer, sem],
            device_id=device,
            device_id_type=MESH,
        )

    def go(copy):
        copy.start()
        pending.append((None, copy))

    def drain():
        for needed, copy in pending:
            if needed is None:
                copy.wait_send()
            else:

                @pl.when(needed)
                def _(copy=copy):
                    copy.wait_send()

        pending.clear()

    def span(chunk):
        return pl.ds(chunk * BLK, BLK)

    def gather_own(held, layer, base, chunk):
        piece = held.at[tp, span(chunk)]
        go(send(piece, piece, layer, base + 8 * chunk, z_partner))
        for d in (1, 3, 2):
            go(send(piece, piece, layer, base + 8 * chunk + d, at_tp(d)))

    def gather_pass(held, layer, base, chunk):
        piece = held.at[other, span(chunk)]
        send(piece, piece, layer, base + 8 * chunk, z_partner).wait_recv()
        for d in (1, 3, 2):
            go(send(piece, piece, layer, base + 8 * chunk + 3 + d, at_tp(d)))

    def gather_end(held, layer, base, chunk):
        piece = held.at[tp, span(chunk)]
        for d in (1, 3, 2):
            send(piece, piece, layer, base + 8 * chunk + d, at_tp(d)).wait_recv()
        for d in (1, 3, 2):
            send(piece, piece, layer, base + 8 * chunk + 3 + d, at_tp(d)).wait_recv()

    def whole_rows(held, chunk):
        return jnp.concatenate([held[i, span(chunk), :] for i in range(8)], axis=1)

    def out_half(layer, number):
        return wo.at[layer, pl.ds(pl.multiple_of(number * BLK + core * (BLK // 2), 64), BLK // 2)]

    def out_cross(layer):
        weights[layer].wait()
        go(send(out_half(layer, tp), out_half(layer, tp), layer, OUT_W, z_partner))

    def out_own(layer):
        for d in (1, 3, 2):
            go(send(out_half(layer, tp), out_half(layer, tp), layer, OUT_W + d, at_tp(d)))

    def out_core(layer, number, sem):
        go(send(out_half(layer, number), out_half(layer, number), layer, OUT_W + 8 + sem, core_partner))

    def out_pass(layer):
        send(out_half(layer, tp), out_half(layer, tp), layer, OUT_W, z_partner).wait_recv()
        for d in (1, 3, 2):
            go(send(out_half(layer, other), out_half(layer, other), layer, OUT_W + 3 + d, at_tp(d)))
        out_core(layer, other, 0)

    def out_share(layer):
        for d in (1, 3, 2):
            held = out_half(layer, tp)
            send(held, held, layer, OUT_W + d, at_tp(d)).wait_recv()
            out_core(layer, (high + 4 - d) % 4 * 2 + low, d)
            send(held, held, layer, OUT_W + 3 + d, at_tp(d)).wait_recv()
            out_core(layer, (high + 4 - d) % 4 * 2 + 1 - low, 3 + d)

    def out_end(layer):
        held = out_half(layer, tp)
        for i in range(7):
            send(held, held, layer, OUT_W + 8 + i, core_partner).wait_recv()

    def start_layer(layer, chunk):
        inputs[layer, tp, span(chunk), :] = stream[span(chunk), :].astype(jnp.bfloat16)
        gather_own(inputs.at[layer], layer, AG_X, chunk)

    def pass_layer(layer, chunk):
        gather_pass(inputs.at[layer], layer, AG_X, chunk)

    def project(layer, chunk):
        gather_end(inputs.at[layer], layer, AG_X, chunk)
        held_kv = (kv_first, kv_second)[layer]
        at = span(chunk)
        normed = normalize(
            whole_rows(inputs.at[layer], chunk).astype(jnp.float32),
            gain_before_ref[layer].astype(jnp.float32),
        )
        cosine, sine = cosine_ref[at, :], sine_ref[at, :]
        here = (8 + core * 4 + col) * blocks + chunk
        held_kv[here, :, 0:BLK] = rotate(
            jnp.dot(normed, wk[layer], preferred_element_type=jnp.float32), cosine, sine
        ).astype(jnp.bfloat16)
        held_kv[here, :, BLK : 2 * BLK] = jnp.dot(
            normed, wv[layer], preferred_element_type=jnp.float32
        ).astype(jnp.bfloat16)
        if chunk % UNIT == UNIT - 1:
            spread_own(layer, chunk // UNIT)
        turned = rotate(
            jnp.dot(normed, wq[layer], preferred_element_type=jnp.float32), cosine, sine
        ).astype(jnp.bfloat16)
        query[at, :] = turned * jnp.bfloat16(HEAD_DIM**-0.5)
        if chunk == blocks - 1:
            out_own(layer)
            out_pass(layer)

    def kv_unit(layer, offset, source, unit):
        number = (offset * 8 + core * 4 + source) * blocks + unit * UNIT
        return (kv_first, kv_second)[layer].at[pl.ds(number, UNIT)]

    def kv_send(layer, unit, kind, source, device, slot=None):
        slot = 1 if slot is None else slot
        target = {KV_FULL: 2 - 2 * core, KV_PART: 2 * core}.get(kind, slot)
        return send(
            kv_unit(layer, slot, source, unit),
            kv_unit(layer, target, source, unit),
            layer,
            KV + unit * KV_SEMS + kind + source,
            device,
        )

    def spread_shard(layer, unit, source):
        kv_send(layer, unit, KV_FULL, source, x_full).start()
        kv_send(layer, unit, KV_CORE, source, core_partner).start()
        pending.append((None, kv_send(layer, unit, KV_FULL, source, x_full)))
        pending.append((None, kv_send(layer, unit, KV_CORE, source, core_partner)))

    def spread_own(layer, unit):
        for kind, device, needed in ((KV_UP, z_up, col < 3), (KV_DOWN, z_down, col > 0)):
            copy = kv_send(layer, unit, kind, col, device)

            @pl.when(needed)
            def _(copy=copy):
                copy.start()

            pending.append((needed, copy))
        spread_shard(layer, unit, col)

    def spread_next(layer, unit, step):
        for kind, source, device, here, onward, part in (
            (KV_UP, col - step, z_up, col >= step, col < 3, core == 1),
            (KV_DOWN, col + step, z_down, col + step <= 3, col > 0, core == 0),
        ):
            arrived = kv_send(layer, unit, kind, source, device)
            aside = kv_send(layer, unit, KV_PART, source, x_part)
            full = kv_send(layer, unit, KV_FULL, source, x_full)
            across = kv_send(layer, unit, KV_CORE, source, core_partner)

            @pl.when(here)
            def _(arrived=arrived, aside=aside, full=full, across=across, onward=onward, part=part):
                arrived.wait_recv()

                @pl.when(onward)
                def _():
                    arrived.start()

                full.start()

                @pl.when(part)
                def _():
                    aside.start()

                across.start()

            pending.append((here & onward, arrived))
            pending.append((here & part, aside))
            pending.append((here, full))
            pending.append((here, across))

    def order_of(step):
        return (col + step) % 4

    def spread_back(layer, unit):
        for step in (0, 1, 3, 2):
            source = order_of(step)
            kv_send(layer, unit, KV_FULL, source, x_full).wait_recv()
            go(kv_send(layer, unit, KV_BACK, source, core_partner, slot=2 - 2 * core))

    def spread_end(layer, unit):
        for step in (1, 2, 3):
            source = order_of(step)

            @pl.when(((core == 0) & (source > col)) | ((core == 1) & (source < col)))
            def _(source=source):
                kv_send(layer, unit, KV_PART, source, x_part).wait_recv()

        for source in range(4):
            kv_send(layer, unit, KV_CORE, source, core_partner).wait_recv()
            kv_send(layer, unit, KV_BACK, source, core_partner).wait_recv()

    lane = lax.broadcasted_iota(jnp.int32, (BLK, BLK), 1)
    chunks = WINDOW * BLK // CHUNK
    each = CHUNK // BLK

    def attend(layer, block):
        held_kv = (kv_first, kv_second)[layer]

        def keys_of(begin, chunk, lanes):
            return jnp.concatenate(
                [held_kv[begin + chunk * each + i][:, lanes : lanes + BLK] for i in range(each)], axis=0
            )

        at = span(block)
        begin = window_ref[block, 0]
        shift = window_ref[block, 1]
        filled = window_ref[block, 2]
        turned = query[at, :]
        zero = jnp.zeros_like(turned)
        stacked = jnp.concatenate(
            [jnp.where(lane < HEAD_DIM, turned, zero), jnp.where(lane < HEAD_DIM, zero, turned)],
            axis=0,
        )
        best = jnp.full((2 * BLK, BLK), masked, jnp.float32)
        for chunk in range(chunks):
            found = lax.dot_general(
                stacked,
                keys_of(begin, chunk, 0),
                (((1,), (1,)), ((), ())),
                preferred_element_type=jnp.float32,
            )
            slot = lax.broadcasted_iota(jnp.int32, (1, CHUNK), 1) + (shift + chunk * CHUNK)
            found = jnp.where((slot >= 0) & (slot < filled), found, masked)
            scores[:, chunk * CHUNK : (chunk + 1) * CHUNK] = found
            for part in range(each):
                best = jnp.maximum(best, found[:, part * BLK : (part + 1) * BLK])
        top = jnp.max(best, axis=1, keepdims=True)
        total = jnp.zeros((2 * BLK, BLK), jnp.float32)
        mixed = jnp.zeros((2 * BLK, BLK), jnp.float32)
        for chunk in range(chunks):
            raised = jnp.exp(scores[:, chunk * CHUNK : (chunk + 1) * CHUNK] - top)
            for part in range(each):
                total = total + raised[:, part * BLK : (part + 1) * BLK]
            mixed = mixed + jnp.dot(
                raised.astype(jnp.bfloat16),
                keys_of(begin, chunk, BLK),
                preferred_element_type=jnp.float32,
            )
        mixed = mixed / jnp.sum(total, axis=1, keepdims=True)
        mixes[layer, tp, at, :] = jnp.where(lane < HEAD_DIM, mixed[0:BLK], mixed[BLK:]).astype(
            jnp.bfloat16
        )
        gather_own(mixes.at[layer], layer, AG_A, block)

    def pass_mix(layer, chunk):
        gather_pass(mixes.at[layer], layer, AG_A, chunk)

    def feed(layer, chunk):
        if chunk == 0:
            out_end(layer)
        gather_end(mixes.at[layer], layer, AG_A, chunk)
        at = span(chunk)
        headed = jnp.dot(
            whole_rows(mixes.at[layer], chunk), wo[layer], preferred_element_type=jnp.float32
        )
        for i in range(8):
            head_part[i] = headed[:, i * BLK : (i + 1) * BLK]
        stream[at, :] = stream[at, :] + head_part[tp]
        middle = whole_rows(inputs.at[layer], chunk).astype(jnp.float32) + headed
        post = normalize(middle, gain_after_ref[layer].astype(jnp.float32))
        gate = jnp.dot(post, wg[layer], preferred_element_type=jnp.float32)
        up = jnp.dot(post, wu[layer], preferred_element_type=jnp.float32)
        hidden = (gate / (1.0 + jnp.exp(-gate)) * up).astype(jnp.bfloat16)
        part = jnp.dot(hidden, wd[layer], preferred_element_type=jnp.float32)
        for i in range(8):
            parts[layer, i, at, :] = part[:, i * BLK : (i + 1) * BLK].astype(jnp.bfloat16)
        for d in (1, 3, 2):
            go(sum_send(layer, chunk, d))
        if chunk == 0 and layer + 1 < layers:
            out_cross(layer + 1)

    def sum_send(layer, chunk, d):
        return send(
            parts.at[layer, pl.ds((high + d) % 4 * 2, 2), span(chunk)],
            parts_in.at[layer, d - 1, pl.ds(0, 2), span(chunk)],
            layer,
            RS_Y + 4 * chunk + d,
            at_tp(d),
        )

    def cross_send(layer, chunk):
        return send(
            half_out.at[layer, span(chunk)],
            half_in.at[layer, span(chunk)],
            layer,
            RS_Y + 4 * chunk,
            z_partner,
        )

    def add_up(layer, chunk):
        at = span(chunk)
        for d in (1, 3, 2):
            sum_send(layer, chunk, d).wait_recv()

        def summed(half):
            total = parts[layer, high * 2 + half, at, :].astype(jnp.float32)
            for d in range(3):
                total = total + parts_in[layer, d, half, at, :].astype(jnp.float32)
            return total

        half_out[layer, at, :] = summed(1 - low).astype(jnp.bfloat16)
        go(cross_send(layer, chunk))
        stream[at, :] = stream[at, :] + summed(low)

    def finish(layer, chunk):
        at = span(chunk)
        cross_send(layer, chunk).wait_recv()
        stream[at, :] = stream[at, :] + half_in[layer, at, :].astype(jnp.float32)
        if layer + 1 < layers:
            start_layer(layer + 1, chunk)

    def in_units(stage):
        def run(layer, chunk):
            if chunk % UNIT == UNIT - 1:
                stage(layer, chunk // UNIT)

        return run

    def wavefront(stages):
        for step in range(blocks + len(stages) - 1):
            for i in reversed(range(len(stages))):
                if 0 <= step - i < blocks:
                    layer, stage = stages[i]
                    stage(layer, step - i)

    def chain(step):
        return in_units(lambda layer, unit: spread_next(layer, unit, step))

    def front(layer):
        return [
            (layer, pass_layer),
            (layer, project),
            (layer, chain(1)),
            (layer, chain(2)),
            (layer, chain(3)),
            (layer, in_units(spread_back)),
        ]

    def rest(layer):
        return [(layer, attend), (layer, pass_mix), (layer, feed), (layer, add_up), (layer, finish)]

    stream[...] = tokens_ref[...].astype(jnp.float32)
    for chunk in range(blocks):
        start_layer(0, chunk)
    out_cross(0)
    for copy in weights[layers:]:
        copy.wait()
    wavefront(front(0))
    for layer in range(layers):
        out_share(layer)
        for unit in range(blocks // UNIT):
            spread_end(layer, unit)
        wavefront(rest(layer) + (front(layer + 1) if layer + 1 < layers else []))
    out_ref[...] = stream[...]
    drain()


def local(
    tokens,
    norm_before,
    query_weight,
    key_weight,
    value_weight,
    output_weight,
    norm_after,
    gate_weight,
    up_weight,
    down_weight,
    block_image,
    image_width,
):
    rows = tokens.shape[0]
    blocks = rows // BLK
    layers = query_weight.shape[0]
    place = lax.axis_index(("row", "col"))
    first, width, filled = [
        lax.dynamic_slice_in_dim(table, place * blocks, blocks)
        for table in block_tables(block_image, image_width)
    ]
    cosine, sine = rope_tables(first, width, place * blocks, blocks)
    origin = (place // 8 - 1) * 8 * blocks
    begin = jnp.minimum(first, place * blocks + 8 * blocks - WINDOW)
    window = jnp.stack([begin - origin, (begin - first) * BLK, filled], axis=1)
    hbm = pl.BlockSpec(memory_space=pl.ANY)
    vmem = pl.BlockSpec(memory_space=pltpu.VMEM)
    bf16, f32 = jnp.bfloat16, jnp.float32
    return pl.pallas_call(
        functools.partial(layers_kernel, layers),
        out_shape=jax.ShapeDtypeStruct(tokens.shape, f32),
        in_specs=[pl.BlockSpec(memory_space=pltpu.SMEM)] + [vmem] * 5 + [hbm] * 7,
        out_specs=vmem,
        scratch_shapes=[
            pltpu.VMEM(query_weight.shape, bf16),
            pltpu.VMEM(key_weight.shape, bf16),
            pltpu.VMEM(value_weight.shape, bf16),
            pltpu.VMEM((layers, 8 * BLK, 8 * BLK), bf16),
            pltpu.VMEM(gate_weight.shape, bf16),
            pltpu.VMEM(up_weight.shape, bf16),
            pltpu.VMEM(down_weight.shape, bf16),
            pltpu.VMEM((layers, 8, rows, BLK), bf16),
            pltpu.VMEM((layers, 8, rows, BLK), bf16),
            pltpu.VMEM((24 * blocks, BLK, 2 * BLK), bf16),
            pltpu.VMEM((24 * blocks, BLK, 2 * BLK), bf16),
            pltpu.VMEM((rows, BLK), bf16),
            pltpu.VMEM((2 * BLK, WINDOW * BLK), f32),
            pltpu.VMEM((8, BLK, BLK), f32),
            pltpu.VMEM((layers, 8, rows, BLK), bf16),
            pltpu.VMEM((layers, 3, 2, rows, BLK), bf16),
            pltpu.VMEM((layers, rows, BLK), bf16),
            pltpu.VMEM((layers, rows, BLK), bf16),
            pltpu.VMEM((rows, BLK), f32),
            pltpu.SemaphoreType.DMA((layers + 6,)),
            pltpu.SemaphoreType.DMA((layers, SEMS)),
            pltpu.SemaphoreType.DMA((layers, SEMS)),
        ],
        compiler_params=pltpu.CompilerParams(
            collective_id=0, has_side_effects=True, vmem_limit_bytes=56 << 20
        ),
        name="encoder_layers",
    )(
        window,
        tokens,
        cosine,
        sine,
        norm_before[:, None, :],
        norm_after[:, None, :],
        query_weight,
        key_weight,
        value_weight,
        output_weight,
        gate_weight,
        up_weight,
        down_weight,
    )


def solution(mesh):
    placed = (
        P(("row", "col"), "tp"),
        P(),
        P(None, None, "tp"),
        P(None, None, "tp"),
        P(None, None, "tp"),
        P(None, "tp", None),
        P(),
        P(None, None, "tp"),
        P(None, None, "tp"),
        P(None, "tp", None),
        P(),
        P(),
    )
    return jax.shard_map(
        local, mesh=mesh, in_specs=placed, out_specs=P(("row", "col"), "tp"), check_vma=False
    )
```

```python
import functools

import jax
import jax.numpy as jnp
import numpy as np
from jax import lax
from jax.experimental import pallas as pl
from jax.experimental.pallas import tpu as pltpu
from jax.sharding import PartitionSpec as P

HEAD_DIM = 64
BLK = 128
WINDOW = 30
CHUNK = 256

epsilon = 1e-05
theta = 10000.0
masked = -1e30
MESH = pl.DeviceIdType.MESH

UNIT = 2

AG_X, AG_A, RS_Y, OUT_W, KV = 0, 32, 64, 80, 96
KV_UP, KV_DOWN, KV_FULL, KV_PART, KV_CORE, KV_BACK, KV_SEMS = 0, 4, 8, 12, 16, 20, 24
SEMS = KV + 2 * KV_SEMS


def frequencies():
    half = HEAD_DIM // 2
    each = theta ** (-2.0 * np.arange(half, dtype=np.float64) / HEAD_DIM)
    return np.tile(np.concatenate([each[0::2], each[1::2]]), 4)[None, :].astype(np.float32)


def normalize(values, gain):
    scale = lax.rsqrt(jnp.mean(values * values, axis=-1, keepdims=True) + epsilon)
    return (values * scale * gain).astype(jnp.bfloat16)


def rotate(heads, cosine, sine):
    lane = lax.broadcasted_iota(jnp.int32, heads.shape, 1)
    front = lax.rem(lane, HEAD_DIM) < HEAD_DIM // 2
    width = heads.shape[1]
    other = jnp.where(
        front,
        pltpu.roll(heads, width - HEAD_DIM // 2, 1),
        pltpu.roll(heads, HEAD_DIM // 2, 1),
    )
    return heads * cosine + other * sine


def tables_kernel(image_ref, width_ref, frequency_ref, window_ref, cosines, sines):
    blocks = window_ref.shape[0]
    row, col = lax.axis_index("row"), lax.axis_index("col")
    first_block = (row * 4 + col) * blocks
    own_images = [image_ref[first_block + block] for block in range(blocks)]

    def tally(i, found):
        image = image_ref[i]
        return tuple(n + jnp.where(image == own, 1, 0) for n, own in zip(found, own_images)) + tuple(
            n + jnp.where(image < own, 1, 0) for n, own in zip(found[blocks:], own_images)
        )

    found = lax.fori_loop(0, image_ref.shape[0], tally, (jnp.int32(0),) * (2 * blocks), unroll=8)
    lane = lax.broadcasted_iota(jnp.int32, (BLK, BLK), 1)
    by_row = lax.rem(lane, HEAD_DIM // 2) < HEAD_DIM // 4
    for block in range(blocks):
        count, first = found[block], found[blocks + block]
        width = width_ref[own_images[block]]
        begin = jnp.clip(first, first_block - 7 * blocks, first_block + 8 * blocks - WINDOW)
        window_ref[block, 0] = begin - (row // 2 - 1) * 8 * blocks
        window_ref[block, 1] = (begin - first) * BLK
        window_ref[block, 2] = lax.div(count * BLK, width) * width
        slot = (
            lax.broadcasted_iota(jnp.int32, (BLK, BLK), 0) + (first_block + block - first) * BLK
        ).astype(jnp.float32)
        wide = jnp.full((BLK, BLK), width, jnp.int32).astype(jnp.float32)
        patch_row = jnp.floor((slot + 0.5) / wide)
        angle = jnp.where(by_row, patch_row, slot - patch_row * wide) * frequency_ref[...]
        cosine, sine = jnp.cos(angle), jnp.sin(angle)
        cosines[block * BLK : (block + 1) * BLK, :] = cosine
        sines[block * BLK : (block + 1) * BLK, :] = jnp.where(
            lax.rem(lane, HEAD_DIM) < HEAD_DIM // 2, -sine, sine
        )


def layers_kernel(
    layers,
    window_ref,
    tokens_ref,
    cosines,
    sines,
    gain_before_ref,
    gain_after_ref,
    wq_hbm,
    wk_hbm,
    wv_hbm,
    wo_hbm,
    wg_hbm,
    wu_hbm,
    wd_hbm,
    out_ref,
    wq,
    wk,
    wv,
    wo,
    wg,
    wu,
    wd,
    inputs,
    mixes,
    kv_first,
    kv_second,
    query,
    scores,
    head_part,
    parts,
    parts_in,
    half_out,
    half_in,
    stream,
    weight_sem,
    send_sem,
    recv_sem,
):
    rows = tokens_ref.shape[0]
    blocks = rows // BLK
    row, col, tp = lax.axis_index("row"), lax.axis_index("col"), lax.axis_index("tp")
    high, low = tp // 2, tp % 2
    chip, core = row // 2, row % 2
    other = high * 2 + 1 - low

    def at_tp(step):
        return (row, col, (high + step) % 4 * 2 + low)

    z_partner = (row, col, other)
    core_partner = (chip * 2 + 1 - core, col, tp)
    x_full = ((row + 6 + 4 * core) % 8, col, tp)
    x_part = ((row + 2 + 4 * core) % 8, col, tp)
    z_up = (row, (col + 1) % 4, tp)
    z_down = (row, (col + 3) % 4, tp)

    barrier = pltpu.get_barrier_semaphore()
    peers = [at_tp(1), at_tp(2), at_tp(3), z_partner, core_partner, x_full, x_part, z_up, z_down]
    for peer in peers:
        pl.semaphore_signal(barrier, inc=1, device_id=peer, device_id_type=MESH)
    pl.semaphore_wait(barrier, len(peers))

    def weight(number, layer, src, dst):
        return pltpu.make_async_copy(src.at[layer], dst, weight_sem.at[number, layer])

    own_out_rows = pl.ds(pl.multiple_of(tp * BLK, BLK), BLK)

    def weights_in(layer):
        return [
            weight(i, layer, src, dst[layer])
            for i, (src, dst) in enumerate([(wk_hbm, wk), (wv_hbm, wv), (wq_hbm, wq)])
        ]

    def weights_out(layer):
        return weight(3, layer, wo_hbm, wo[layer].at[own_out_rows])

    def weights_feed(layer):
        return [
            weight(4 + i, layer, src, dst[layer])
            for i, (src, dst) in enumerate([(wg_hbm, wg), (wu_hbm, wu), (wd_hbm, wd)])
        ]

    pending = []

    def send(src, dst, layer, sem, device):
        return pltpu.make_async_remote_copy(
            src_ref=src,
            dst_ref=dst,
            send_sem=send_sem.at[layer, sem],
            recv_sem=recv_sem.at[layer, sem],
            device_id=device,
            device_id_type=MESH,
        )

    def go(copy):
        copy.start()
        pending.append((None, copy))

    def drain():
        for needed, copy in pending:
            if needed is None:
                copy.wait_send()
            else:

                @pl.when(needed)
                def _(copy=copy):
                    copy.wait_send()

        pending.clear()

    def span(chunk):
        return pl.ds(chunk * BLK, BLK)

    def gather_own(held, layer, base, chunk):
        piece = held.at[tp, span(chunk)]
        go(send(piece, piece, layer, base + 8 * chunk, z_partner))
        for d in (1, 3, 2):
            go(send(piece, piece, layer, base + 8 * chunk + d, at_tp(d)))

    def gather_pass(held, layer, base, chunk):
        piece = held.at[other, span(chunk)]
        send(piece, piece, layer, base + 8 * chunk, z_partner).wait_recv()
        for d in (1, 3, 2):
            go(send(piece, piece, layer, base + 8 * chunk + 3 + d, at_tp(d)))

    def gather_end(held, layer, base, chunk):
        piece = held.at[tp, span(chunk)]
        for d in (1, 3, 2):
            send(piece, piece, layer, base + 8 * chunk + d, at_tp(d)).wait_recv()
        for d in (1, 3, 2):
            send(piece, piece, layer, base + 8 * chunk + 3 + d, at_tp(d)).wait_recv()

    def whole_rows(held, chunk):
        return jnp.concatenate([held[i, span(chunk), :] for i in range(8)], axis=1)

    def out_half(layer, number):
        return wo[layer].at[pl.ds(pl.multiple_of(number * BLK + core * (BLK // 2), 64), BLK // 2)]

    def out_cross(layer):
        weights_out(layer).wait()
        go(send(out_half(layer, tp), out_half(layer, tp), layer, OUT_W, z_partner))

    def out_own(layer):
        for d in (1, 3, 2):
            go(send(out_half(layer, tp), out_half(layer, tp), layer, OUT_W + d, at_tp(d)))

    def out_core(layer, number, sem):
        go(send(out_half(layer, number), out_half(layer, number), layer, OUT_W + 8 + sem, core_partner))

    def out_pass(layer):
        send(out_half(layer, tp), out_half(layer, tp), layer, OUT_W, z_partner).wait_recv()
        for d in (1, 3, 2):
            go(send(out_half(layer, other), out_half(layer, other), layer, OUT_W + 3 + d, at_tp(d)))
        out_core(layer, other, 0)

    def out_share(layer):
        for d in (1, 3, 2):
            held = out_half(layer, tp)
            send(held, held, layer, OUT_W + d, at_tp(d)).wait_recv()
            out_core(layer, (high + 4 - d) % 4 * 2 + low, d)
            send(held, held, layer, OUT_W + 3 + d, at_tp(d)).wait_recv()
            out_core(layer, (high + 4 - d) % 4 * 2 + 1 - low, 3 + d)

    def out_end(layer):
        held = out_half(layer, tp)
        for i in range(7):
            send(held, held, layer, OUT_W + 8 + i, core_partner).wait_recv()

    def start_layer(layer, chunk):
        inputs[layer, tp, span(chunk), :] = stream[span(chunk), :].astype(jnp.bfloat16)
        gather_own(inputs.at[layer], layer, AG_X, chunk)

    def pass_layer(layer, chunk):
        gather_pass(inputs.at[layer], layer, AG_X, chunk)

    def project(layer, chunk):
        gather_end(inputs.at[layer], layer, AG_X, chunk)
        if chunk == 0:
            for copy in weights_in(layer):
                copy.wait()
        held_kv = (kv_first, kv_second)[layer]
        at = span(chunk)
        normed = normalize(
            whole_rows(inputs.at[layer], chunk).astype(jnp.float32),
            gain_before_ref[...].astype(jnp.float32)[layer : layer + 1],
        )
        cosine, sine = cosines[at, :], sines[at, :]
        here = (8 + core * 4 + col) * blocks + chunk
        held_kv[here, :, 0:BLK] = rotate(
            jnp.dot(normed, wk[layer][...], preferred_element_type=jnp.float32), cosine, sine
        ).astype(jnp.bfloat16)
        held_kv[here, :, BLK : 2 * BLK] = jnp.dot(
            normed, wv[layer][...], preferred_element_type=jnp.float32
        ).astype(jnp.bfloat16)
        if chunk % UNIT == UNIT - 1:
            spread_own(layer, chunk // UNIT)
        turned = rotate(
            jnp.dot(normed, wq[layer][...], preferred_element_type=jnp.float32), cosine, sine
        ).astype(jnp.bfloat16)
        query[at, :] = turned * jnp.bfloat16(HEAD_DIM**-0.5)
        if chunk == blocks - 1:
            out_own(layer)
            out_pass(layer)
            if layer == 0:
                for copy in weights_feed(0):
                    copy.start()
                for later in range(1, layers):
                    for copy in weights_in(later) + [weights_out(later)] + weights_feed(later):
                        copy.start()

    def kv_unit(layer, offset, source, unit):
        number = (offset * 8 + core * 4 + source) * blocks + unit * UNIT
        return (kv_first, kv_second)[layer].at[pl.ds(number, UNIT)]

    def kv_send(layer, unit, kind, source, device, slot=None):
        slot = 1 if slot is None else slot
        target = {KV_FULL: 2 - 2 * core, KV_PART: 2 * core}.get(kind, slot)
        return send(
            kv_unit(layer, slot, source, unit),
            kv_unit(layer, target, source, unit),
            layer,
            KV + unit * KV_SEMS + kind + source,
            device,
        )

    def spread_shard(layer, unit, source):
        kv_send(layer, unit, KV_FULL, source, x_full).start()
        kv_send(layer, unit, KV_CORE, source, core_partner).start()
        pending.append((None, kv_send(layer, unit, KV_FULL, source, x_full)))
        pending.append((None, kv_send(layer, unit, KV_CORE, source, core_partner)))

    def spread_own(layer, unit):
        for kind, device, needed in ((KV_UP, z_up, col < 3), (KV_DOWN, z_down, col > 0)):
            copy = kv_send(layer, unit, kind, col, device)

            @pl.when(needed)
            def _(copy=copy):
                copy.start()

            pending.append((needed, copy))
        spread_shard(layer, unit, col)

    def spread_next(layer, unit, step):
        for kind, source, device, here, onward, part in (
            (KV_UP, col - step, z_up, col >= step, col < 3, core == 1),
            (KV_DOWN, col + step, z_down, col + step <= 3, col > 0, core == 0),
        ):
            arrived = kv_send(layer, unit, kind, source, device)
            aside = kv_send(layer, unit, KV_PART, source, x_part)
            full = kv_send(layer, unit, KV_FULL, source, x_full)
            across = kv_send(layer, unit, KV_CORE, source, core_partner)

            @pl.when(here)
            def _(arrived=arrived, aside=aside, full=full, across=across, onward=onward, part=part):
                arrived.wait_recv()

                @pl.when(onward)
                def _():
                    arrived.start()

                full.start()

                @pl.when(part)
                def _():
                    aside.start()

                across.start()

            pending.append((here & onward, arrived))
            pending.append((here & part, aside))
            pending.append((here, full))
            pending.append((here, across))

    def order_of(step):
        return (col + step) % 4

    def spread_back(layer, unit):
        for step in (0, 1, 3, 2):
            source = order_of(step)
            kv_send(layer, unit, KV_FULL, source, x_full).wait_recv()
            go(kv_send(layer, unit, KV_BACK, source, core_partner, slot=2 - 2 * core))

    def spread_end(layer, unit):
        for step in (1, 2, 3):
            source = order_of(step)

            @pl.when(((core == 0) & (source > col)) | ((core == 1) & (source < col)))
            def _(source=source):
                kv_send(layer, unit, KV_PART, source, x_part).wait_recv()

        for source in range(4):
            kv_send(layer, unit, KV_CORE, source, core_partner).wait_recv()
            kv_send(layer, unit, KV_BACK, source, core_partner).wait_recv()

    lane = lax.broadcasted_iota(jnp.int32, (BLK, BLK), 1)
    chunks = WINDOW * BLK // CHUNK
    each = CHUNK // BLK

    def attend(layer, block):
        held_kv = (kv_first, kv_second)[layer]

        def keys_of(begin, chunk, lanes):
            return jnp.concatenate(
                [held_kv[begin + chunk * each + i][:, lanes : lanes + BLK] for i in range(each)], axis=0
            )

        at = span(block)
        begin = window_ref[block, 0]
        shift = window_ref[block, 1]
        filled = window_ref[block, 2]
        turned = query[at, :]
        zero = jnp.zeros_like(turned)
        stacked = jnp.concatenate(
            [jnp.where(lane < HEAD_DIM, turned, zero), jnp.where(lane < HEAD_DIM, zero, turned)],
            axis=0,
        )
        best = jnp.full((2 * BLK, BLK), masked, jnp.float32)
        for chunk in range(chunks):
            found = lax.dot_general(
                stacked,
                keys_of(begin, chunk, 0),
                (((1,), (1,)), ((), ())),
                preferred_element_type=jnp.float32,
            )
            slot = lax.broadcasted_iota(jnp.int32, (1, CHUNK), 1) + (shift + chunk * CHUNK)
            found = jnp.where((slot >= 0) & (slot < filled), found, masked)
            scores[:, chunk * CHUNK : (chunk + 1) * CHUNK] = found
            for part in range(each):
                best = jnp.maximum(best, found[:, part * BLK : (part + 1) * BLK])
        top = jnp.max(best, axis=1, keepdims=True)
        total = jnp.zeros((2 * BLK, BLK), jnp.float32)
        mixed = jnp.zeros((2 * BLK, BLK), jnp.float32)
        for chunk in range(chunks):
            raised = jnp.exp(scores[:, chunk * CHUNK : (chunk + 1) * CHUNK] - top)
            for part in range(each):
                total = total + raised[:, part * BLK : (part + 1) * BLK]
            mixed = mixed + jnp.dot(
                raised.astype(jnp.bfloat16),
                keys_of(begin, chunk, BLK),
                preferred_element_type=jnp.float32,
            )
        mixed = mixed / jnp.sum(total, axis=1, keepdims=True)
        mixes[layer, tp, at, :] = jnp.where(lane < HEAD_DIM, mixed[0:BLK], mixed[BLK:]).astype(
            jnp.bfloat16
        )
        gather_own(mixes.at[layer], layer, AG_A, block)

    def pass_mix(layer, chunk):
        gather_pass(mixes.at[layer], layer, AG_A, chunk)

    def feed(layer, chunk):
        if chunk == 0:
            out_end(layer)
            for copy in weights_feed(layer):
                copy.wait()
        gather_end(mixes.at[layer], layer, AG_A, chunk)
        at = span(chunk)
        headed = jnp.dot(
            whole_rows(mixes.at[layer], chunk), wo[layer][...], preferred_element_type=jnp.float32
        )
        for i in range(8):
            head_part[i] = headed[:, i * BLK : (i + 1) * BLK]
        stream[at, :] = stream[at, :] + head_part[tp]
        middle = whole_rows(inputs.at[layer], chunk).astype(jnp.float32) + headed
        post = normalize(middle, gain_after_ref[...].astype(jnp.float32)[layer : layer + 1])
        gate = jnp.dot(post, wg[layer][...], preferred_element_type=jnp.float32)
        up = jnp.dot(post, wu[layer][...], preferred_element_type=jnp.float32)
        hidden = (gate / (1.0 + jnp.exp(-gate)) * up).astype(jnp.bfloat16)
        part = jnp.dot(hidden, wd[layer][...], preferred_element_type=jnp.float32)
        for i in range(8):
            parts[layer, i, at, :] = part[:, i * BLK : (i + 1) * BLK].astype(jnp.bfloat16)
        for d in (1, 3, 2):
            go(sum_send(layer, chunk, d))
        if chunk == 0 and layer + 1 < layers:
            out_cross(layer + 1)

    def sum_send(layer, chunk, d):
        return send(
            parts.at[layer, pl.ds((high + d) % 4 * 2, 2), span(chunk)],
            parts_in.at[layer, d - 1, pl.ds(0, 2), span(chunk)],
            layer,
            RS_Y + 4 * chunk + d,
            at_tp(d),
        )

    def cross_send(layer, chunk):
        return send(
            half_out.at[layer, span(chunk)],
            half_in.at[layer, span(chunk)],
            layer,
            RS_Y + 4 * chunk,
            z_partner,
        )

    def add_up(layer, chunk):
        at = span(chunk)
        for d in (1, 3, 2):
            sum_send(layer, chunk, d).wait_recv()

        def summed(half):
            total = parts[layer, high * 2 + half, at, :].astype(jnp.float32)
            for d in range(3):
                total = total + parts_in[layer, d, half, at, :].astype(jnp.float32)
            return total

        half_out[layer, at, :] = summed(1 - low).astype(jnp.bfloat16)
        go(cross_send(layer, chunk))
        stream[at, :] = stream[at, :] + summed(low)

    def finish(layer, chunk):
        at = span(chunk)
        cross_send(layer, chunk).wait_recv()
        stream[at, :] = stream[at, :] + half_in[layer, at, :].astype(jnp.float32)
        if layer + 1 < layers:
            start_layer(layer + 1, chunk)

    def in_units(stage):
        def run(layer, chunk):
            if chunk % UNIT == UNIT - 1:
                stage(layer, chunk // UNIT)

        return run

    def wavefront(stages):
        for step in range(blocks + len(stages) - 1):
            for i in reversed(range(len(stages))):
                if 0 <= step - i < blocks:
                    layer, stage = stages[i]
                    stage(layer, step - i)

    def chain(step):
        return in_units(lambda layer, unit: spread_next(layer, unit, step))

    def front(layer):
        return [
            (layer, pass_layer),
            (layer, project),
            (layer, chain(1)),
            (layer, chain(2)),
            (layer, chain(3)),
            (layer, in_units(spread_back)),
        ]

    def rest(layer):
        return [(layer, attend), (layer, pass_mix), (layer, feed), (layer, add_up), (layer, finish)]

    stream[...] = tokens_ref[...].astype(jnp.float32)
    for chunk in range(blocks):
        start_layer(0, chunk)
    for copy in weights_in(0) + [weights_out(0)]:
        copy.start()
    out_cross(0)
    wavefront(front(0))
    for layer in range(layers):
        out_share(layer)
        for unit in range(blocks // UNIT):
            spread_end(layer, unit)
        wavefront(rest(layer) + (front(layer + 1) if layer + 1 < layers else []))
    out_ref[...] = stream[...]
    drain()


def local(
    tokens,
    norm_before,
    query_weight,
    key_weight,
    value_weight,
    output_weight,
    norm_after,
    gate_weight,
    up_weight,
    down_weight,
    block_image,
    image_width,
):
    rows = tokens.shape[0]
    blocks = rows // BLK
    layers = query_weight.shape[0]
    hbm = pl.BlockSpec(memory_space=pl.ANY)
    vmem = pl.BlockSpec(memory_space=pltpu.VMEM)
    smem = pl.BlockSpec(memory_space=pltpu.SMEM)
    bf16, f32 = jnp.bfloat16, jnp.float32
    window, cosine, sine = pl.pallas_call(
        tables_kernel,
        out_shape=(
            jax.ShapeDtypeStruct((blocks, 3), jnp.int32),
            jax.ShapeDtypeStruct((rows, BLK), f32),
            jax.ShapeDtypeStruct((rows, BLK), f32),
        ),
        in_specs=[smem, smem, vmem],
        out_specs=(smem, vmem, vmem),
        name="tables",
    )(block_image, image_width, frequencies())
    return pl.pallas_call(
        functools.partial(layers_kernel, layers),
        out_shape=jax.ShapeDtypeStruct(tokens.shape, f32),
        in_specs=[smem] + [vmem] * 5 + [hbm] * 7,
        out_specs=vmem,
        scratch_shapes=[
            [pltpu.VMEM(query_weight.shape[1:], bf16)] * layers,
            [pltpu.VMEM(key_weight.shape[1:], bf16)] * layers,
            [pltpu.VMEM(value_weight.shape[1:], bf16)] * layers,
            [pltpu.VMEM((8 * BLK, 8 * BLK), bf16)] * layers,
            [pltpu.VMEM(gate_weight.shape[1:], bf16)] * layers,
            [pltpu.VMEM(up_weight.shape[1:], bf16)] * layers,
            [pltpu.VMEM(down_weight.shape[1:], bf16)] * layers,
            pltpu.VMEM((layers, 8, rows, BLK), bf16),
            pltpu.VMEM((layers, 8, rows, BLK), bf16),
            pltpu.VMEM((24 * blocks, BLK, 2 * BLK), bf16),
            pltpu.VMEM((24 * blocks, BLK, 2 * BLK), bf16),
            pltpu.VMEM((rows, BLK), bf16),
            pltpu.VMEM((2 * BLK, WINDOW * BLK), f32),
            pltpu.VMEM((8, BLK, BLK), f32),
            pltpu.VMEM((layers, 8, rows, BLK), bf16),
            pltpu.VMEM((layers, 3, 2, rows, BLK), bf16),
            pltpu.VMEM((layers, rows, BLK), bf16),
            pltpu.VMEM((layers, rows, BLK), bf16),
            pltpu.VMEM((rows, BLK), f32),
            pltpu.SemaphoreType.DMA((7, layers)),
            pltpu.SemaphoreType.DMA((layers, SEMS)),
            pltpu.SemaphoreType.DMA((layers, SEMS)),
        ],
        compiler_params=pltpu.CompilerParams(
            collective_id=0, has_side_effects=True, vmem_limit_bytes=56 << 20
        ),
        name="encoder_layers",
    )(
        window,
        tokens,
        cosine,
        sine,
        norm_before,
        norm_after,
        query_weight,
        key_weight,
        value_weight,
        output_weight,
        gate_weight,
        up_weight,
        down_weight,
    )


def solution(mesh):
    placed = (
        P(("row", "col"), "tp"),
        P(),
        P(None, None, "tp"),
        P(None, None, "tp"),
        P(None, None, "tp"),
        P(None, "tp", None),
        P(),
        P(None, None, "tp"),
        P(None, None, "tp"),
        P(None, "tp", None),
        P(),
        P(),
    )
    return jax.shard_map(
        local, mesh=mesh, in_specs=placed, out_specs=P(("row", "col"), "tp"), check_vma=False
    )
```

```python
import functools

import jax
import jax.numpy as jnp
import numpy as np
from jax import lax
from jax.experimental import pallas as pl
from jax.experimental.pallas import tpu as pltpu
from jax.sharding import PartitionSpec as P

HEAD_DIM = 64
BLK = 128
WINDOW = 30
CHUNK = 256

epsilon = 1e-05
theta = 10000.0
masked = -1e30
MESH = pl.DeviceIdType.MESH

LAG = 3
UNIT = 2

AG_X, AG_A, RS_Y, OUT_W, KV = 0, 32, 64, 80, 96
KV_UP, KV_DOWN, KV_FULL, KV_PART, KV_CORE, KV_BACK, KV_SEMS = 0, 4, 8, 12, 16, 20, 24
SEMS = KV + 2 * KV_SEMS


def frequencies():
    half = HEAD_DIM // 2
    each = theta ** (-2.0 * np.arange(half, dtype=np.float64) / HEAD_DIM)
    return np.tile(np.concatenate([each[0::2], each[1::2]]), 4)[None, :].astype(np.float32)


def normalize(values, gain):
    scale = lax.rsqrt(jnp.mean(values * values, axis=-1, keepdims=True) + epsilon)
    return (values * scale * gain).astype(jnp.bfloat16)


def rotate(heads, cosine, sine):
    lane = lax.broadcasted_iota(jnp.int32, heads.shape, 1)
    front = lax.rem(lane, HEAD_DIM) < HEAD_DIM // 2
    width = heads.shape[1]
    other = jnp.where(
        front,
        pltpu.roll(heads, width - HEAD_DIM // 2, 1),
        pltpu.roll(heads, HEAD_DIM // 2, 1),
    )
    return heads * cosine + other * sine


def tables_kernel(image_ref, images_ref, width_ref, frequency_ref, window_ref, cosines, sines):
    blocks = window_ref.shape[0]
    row, col = lax.axis_index("row"), lax.axis_index("col")
    first_block = (row * 4 + col) * blocks
    own_images = [image_ref[first_block + block] for block in range(blocks)]

    images = images_ref[...]
    lane = lax.broadcasted_iota(jnp.int32, (BLK, BLK), 1)
    by_row = lax.rem(lane, HEAD_DIM // 2) < HEAD_DIM // 4
    for block in range(blocks):
        own = own_images[block]
        count = jnp.sum(jnp.where(images == own, 1, 0))
        first = jnp.sum(jnp.where(images < own, 1, 0))
        width = width_ref[own_images[block]]
        begin = jnp.clip(first, first_block - 7 * blocks, first_block + 8 * blocks - WINDOW)
        window_ref[block, 0] = begin - (row // 2 - 1) * 8 * blocks
        window_ref[block, 1] = (begin - first) * BLK
        window_ref[block, 2] = lax.div(count * BLK, width) * width
        slot = (
            lax.broadcasted_iota(jnp.int32, (BLK, BLK), 0) + (first_block + block - first) * BLK
        ).astype(jnp.float32)
        wide = jnp.full((BLK, BLK), width, jnp.int32).astype(jnp.float32)
        patch_row = jnp.floor((slot + 0.5) / wide)
        angle = jnp.where(by_row, patch_row, slot - patch_row * wide) * frequency_ref[...]
        cosine, sine = jnp.cos(angle), jnp.sin(angle)
        cosines[block * BLK : (block + 1) * BLK, :] = cosine
        sines[block * BLK : (block + 1) * BLK, :] = jnp.where(
            lax.rem(lane, HEAD_DIM) < HEAD_DIM // 2, -sine, sine
        )


def layers_kernel(
    layers,
    window_ref,
    tokens_ref,
    cosines,
    sines,
    gain_before_ref,
    gain_after_ref,
    wq_hbm,
    wk_hbm,
    wv_hbm,
    wo_hbm,
    wg_hbm,
    wu_hbm,
    wd_hbm,
    out_ref,
    wq,
    wk,
    wv,
    wo,
    wg,
    wu,
    wd,
    inputs,
    mixes,
    kv_first,
    kv_second,
    query,
    scores,
    head_part,
    parts,
    parts_in,
    half_out,
    half_in,
    stream,
    weight_sem,
    send_sem,
    recv_sem,
):
    rows = tokens_ref.shape[0]
    blocks = rows // BLK
    row, col, tp = lax.axis_index("row"), lax.axis_index("col"), lax.axis_index("tp")
    high, low = tp // 2, tp % 2
    chip, core = row // 2, row % 2
    other = high * 2 + 1 - low

    def at_tp(step):
        return (row, col, (high + step) % 4 * 2 + low)

    z_partner = (row, col, other)
    core_partner = (chip * 2 + 1 - core, col, tp)
    x_full = ((row + 6 + 4 * core) % 8, col, tp)
    x_part = ((row + 2 + 4 * core) % 8, col, tp)
    z_up = (row, (col + 1) % 4, tp)
    z_down = (row, (col + 3) % 4, tp)

    def weight(number, layer, src, dst):
        return pltpu.make_async_copy(src.at[layer], dst, weight_sem.at[number, layer])

    own_out_rows = pl.ds(pl.multiple_of(tp * BLK, BLK), BLK)

    def weights_in(layer):
        return [
            weight(i, layer, src, dst[layer])
            for i, (src, dst) in enumerate([(wk_hbm, wk), (wv_hbm, wv), (wq_hbm, wq)])
        ]

    def weights_out(layer):
        return weight(3, layer, wo_hbm, wo[layer].at[own_out_rows])

    def weights_feed(layer):
        return [
            weight(4 + i, layer, src, dst[layer])
            for i, (src, dst) in enumerate([(wg_hbm, wg), (wu_hbm, wu), (wd_hbm, wd)])
        ]

    for copy in weights_in(0) + [weights_out(0)]:
        copy.start()

    barrier = pltpu.get_barrier_semaphore()
    peers = [at_tp(1), at_tp(2), at_tp(3), z_partner, core_partner, x_full, x_part, z_up, z_down]
    for peer in peers:
        pl.semaphore_signal(barrier, inc=1, device_id=peer, device_id_type=MESH)
    pl.semaphore_wait(barrier, len(peers))

    pending = []

    def send(src, dst, layer, sem, device):
        return pltpu.make_async_remote_copy(
            src_ref=src,
            dst_ref=dst,
            send_sem=send_sem.at[layer, sem],
            recv_sem=recv_sem.at[layer, sem],
            device_id=device,
            device_id_type=MESH,
        )

    def go(copy):
        copy.start()
        pending.append((None, copy))

    def drain():
        for needed, copy in pending:
            if needed is None:
                copy.wait_send()
            else:

                @pl.when(needed)
                def _(copy=copy):
                    copy.wait_send()

        pending.clear()

    def span(chunk):
        return pl.ds(chunk * BLK, BLK)

    def gather_own(held, layer, base, chunk):
        piece = held.at[tp, span(chunk)]
        go(send(piece, piece, layer, base + 8 * chunk, z_partner))
        for d in (1, 3, 2):
            go(send(piece, piece, layer, base + 8 * chunk + d, at_tp(d)))

    def gather_pass(held, layer, base, chunk):
        piece = held.at[other, span(chunk)]
        send(piece, piece, layer, base + 8 * chunk, z_partner).wait_recv()
        for d in (1, 3, 2):
            go(send(piece, piece, layer, base + 8 * chunk + 3 + d, at_tp(d)))

    def gather_end(held, layer, base, chunk):
        piece = held.at[tp, span(chunk)]
        for d in (1, 3, 2):
            send(piece, piece, layer, base + 8 * chunk + d, at_tp(d)).wait_recv()
        for d in (1, 3, 2):
            send(piece, piece, layer, base + 8 * chunk + 3 + d, at_tp(d)).wait_recv()

    def whole_rows(held, chunk):
        return jnp.concatenate([held[i, span(chunk), :] for i in range(8)], axis=1)

    def out_half(layer, number):
        return wo[layer].at[pl.ds(pl.multiple_of(number * BLK + core * (BLK // 2), 64), BLK // 2)]

    def out_cross(layer):
        weights_out(layer).wait()
        go(send(out_half(layer, tp), out_half(layer, tp), layer, OUT_W, z_partner))

    def out_own(layer):
        for d in (1, 3, 2):
            go(send(out_half(layer, tp), out_half(layer, tp), layer, OUT_W + d, at_tp(d)))

    def out_core(layer, number, sem):
        go(send(out_half(layer, number), out_half(layer, number), layer, OUT_W + 8 + sem, core_partner))

    def out_pass(layer):
        send(out_half(layer, tp), out_half(layer, tp), layer, OUT_W, z_partner).wait_recv()
        for d in (1, 3, 2):
            go(send(out_half(layer, other), out_half(layer, other), layer, OUT_W + 3 + d, at_tp(d)))
        out_core(layer, other, 0)

    def out_share(layer):
        for d in (1, 3, 2):
            held = out_half(layer, tp)
            send(held, held, layer, OUT_W + d, at_tp(d)).wait_recv()
            out_core(layer, (high + 4 - d) % 4 * 2 + low, d)
            send(held, held, layer, OUT_W + 3 + d, at_tp(d)).wait_recv()
            out_core(layer, (high + 4 - d) % 4 * 2 + 1 - low, 3 + d)

    def out_end(layer):
        held = out_half(layer, tp)
        for i in range(7):
            send(held, held, layer, OUT_W + 8 + i, core_partner).wait_recv()

    def start_layer(layer, chunk):
        inputs[layer, tp, span(chunk), :] = stream[span(chunk), :].astype(jnp.bfloat16)
        gather_own(inputs.at[layer], layer, AG_X, chunk)

    def pass_layer(layer, chunk):
        gather_pass(inputs.at[layer], layer, AG_X, chunk)

    def project(layer, chunk):
        if layer == 0 and chunk == 0:
            out_cross(0)
        gather_end(inputs.at[layer], layer, AG_X, chunk)
        if chunk == 0:
            for copy in weights_in(layer):
                copy.wait()
        held_kv = (kv_first, kv_second)[layer]
        at = span(chunk)
        normed = normalize(
            whole_rows(inputs.at[layer], chunk).astype(jnp.float32),
            gain_before_ref[...].astype(jnp.float32)[layer : layer + 1],
        )
        cosine, sine = cosines[at, :], sines[at, :]
        here = (8 + core * 4 + col) * blocks + chunk
        held_kv[here, :, 0:BLK] = rotate(
            jnp.dot(normed, wk[layer][...], preferred_element_type=jnp.float32), cosine, sine
        ).astype(jnp.bfloat16)
        held_kv[here, :, BLK : 2 * BLK] = jnp.dot(
            normed, wv[layer][...], preferred_element_type=jnp.float32
        ).astype(jnp.bfloat16)
        if chunk % UNIT == UNIT - 1:
            spread_own(layer, chunk // UNIT)
        turned = rotate(
            jnp.dot(normed, wq[layer][...], preferred_element_type=jnp.float32), cosine, sine
        ).astype(jnp.bfloat16)
        query[at, :] = turned * jnp.bfloat16(HEAD_DIM**-0.5)
        if chunk == blocks - 1:
            out_own(layer)
            out_pass(layer)
            if layer == 0:
                for copy in weights_feed(0):
                    copy.start()
                for later in range(1, layers):
                    for copy in weights_in(later) + [weights_out(later)] + weights_feed(later):
                        copy.start()

    def kv_unit(layer, offset, source, unit):
        number = (offset * 8 + core * 4 + source) * blocks + unit * UNIT
        return (kv_first, kv_second)[layer].at[pl.ds(number, UNIT)]

    def kv_send(layer, unit, kind, source, device, slot=None):
        slot = 1 if slot is None else slot
        target = {KV_FULL: 2 - 2 * core, KV_PART: 2 * core}.get(kind, slot)
        return send(
            kv_unit(layer, slot, source, unit),
            kv_unit(layer, target, source, unit),
            layer,
            KV + unit * KV_SEMS + kind + source,
            device,
        )

    def spread_shard(layer, unit, source):
        kv_send(layer, unit, KV_FULL, source, x_full).start()
        kv_send(layer, unit, KV_CORE, source, core_partner).start()
        pending.append((None, kv_send(layer, unit, KV_FULL, source, x_full)))
        pending.append((None, kv_send(layer, unit, KV_CORE, source, core_partner)))

    def spread_own(layer, unit):
        for kind, device, needed in ((KV_UP, z_up, col < 3), (KV_DOWN, z_down, col > 0)):
            copy = kv_send(layer, unit, kind, col, device)

            @pl.when(needed)
            def _(copy=copy):
                copy.start()

            pending.append((needed, copy))
        spread_shard(layer, unit, col)

    def spread_next(layer, unit, step):
        for kind, source, device, here, onward, part in (
            (KV_UP, col - step, z_up, col >= step, col < 3, core == 1),
            (KV_DOWN, col + step, z_down, col + step <= 3, col > 0, core == 0),
        ):
            arrived = kv_send(layer, unit, kind, source, device)
            aside = kv_send(layer, unit, KV_PART, source, x_part)
            full = kv_send(layer, unit, KV_FULL, source, x_full)
            across = kv_send(layer, unit, KV_CORE, source, core_partner)

            @pl.when(here)
            def _(arrived=arrived, aside=aside, full=full, across=across, onward=onward, part=part):
                arrived.wait_recv()

                @pl.when(onward)
                def _():
                    arrived.start()

                full.start()

                @pl.when(part)
                def _():
                    aside.start()

                across.start()

            pending.append((here & onward, arrived))
            pending.append((here & part, aside))
            pending.append((here, full))
            pending.append((here, across))

    def order_of(step):
        return (col + step) % 4

    def spread_back(layer, unit):
        for step in (0, 1, 3, 2):
            source = order_of(step)
            kv_send(layer, unit, KV_FULL, source, x_full).wait_recv()
            go(kv_send(layer, unit, KV_BACK, source, core_partner, slot=2 - 2 * core))

    def spread_end(layer, unit):
        for step in (1, 2, 3):
            source = order_of(step)

            @pl.when(((core == 0) & (source > col)) | ((core == 1) & (source < col)))
            def _(source=source):
                kv_send(layer, unit, KV_PART, source, x_part).wait_recv()

        for source in range(4):
            kv_send(layer, unit, KV_CORE, source, core_partner).wait_recv()
            kv_send(layer, unit, KV_BACK, source, core_partner).wait_recv()

    lane = lax.broadcasted_iota(jnp.int32, (BLK, BLK), 1)
    chunks = WINDOW * BLK // CHUNK
    each = CHUNK // BLK

    def attend(layer, block):
        held_kv = (kv_first, kv_second)[layer]

        def keys_of(begin, chunk, lanes):
            return jnp.concatenate(
                [held_kv[begin + chunk * each + i][:, lanes : lanes + BLK] for i in range(each)], axis=0
            )

        at = span(block)
        begin = window_ref[block, 0]
        shift = window_ref[block, 1]
        filled = window_ref[block, 2]
        turned = query[at, :]
        zero = jnp.zeros_like(turned)
        stacked = jnp.concatenate(
            [jnp.where(lane < HEAD_DIM, turned, zero), jnp.where(lane < HEAD_DIM, zero, turned)],
            axis=0,
        )
        best = jnp.full((2 * BLK, BLK), masked, jnp.float32)
        for chunk in range(chunks):
            found = lax.dot_general(
                stacked,
                keys_of(begin, chunk, 0),
                (((1,), (1,)), ((), ())),
                preferred_element_type=jnp.float32,
            )
            slot = lax.broadcasted_iota(jnp.int32, (1, CHUNK), 1) + (shift + chunk * CHUNK)
            found = jnp.where((slot >= 0) & (slot < filled), found, masked)
            scores[:, chunk * CHUNK : (chunk + 1) * CHUNK] = found
            for part in range(each):
                best = jnp.maximum(best, found[:, part * BLK : (part + 1) * BLK])
        top = jnp.max(best, axis=1, keepdims=True)
        total = jnp.zeros((2 * BLK, BLK), jnp.float32)
        mixed = jnp.zeros((2 * BLK, BLK), jnp.float32)
        for chunk in range(chunks):
            raised = jnp.exp(scores[:, chunk * CHUNK : (chunk + 1) * CHUNK] - top)
            for part in range(each):
                total = total + raised[:, part * BLK : (part + 1) * BLK]
            mixed = mixed + jnp.dot(
                raised.astype(jnp.bfloat16),
                keys_of(begin, chunk, BLK),
                preferred_element_type=jnp.float32,
            )
        mixed = mixed / jnp.sum(total, axis=1, keepdims=True)
        mixes[layer, tp, at, :] = jnp.where(lane < HEAD_DIM, mixed[0:BLK], mixed[BLK:]).astype(
            jnp.bfloat16
        )
        gather_own(mixes.at[layer], layer, AG_A, block)

    def pass_mix(layer, chunk):
        gather_pass(mixes.at[layer], layer, AG_A, chunk)

    def feed(layer, chunk):
        if chunk == 0:
            out_end(layer)
            for copy in weights_feed(layer):
                copy.wait()
        gather_end(mixes.at[layer], layer, AG_A, chunk)
        at = span(chunk)
        headed = jnp.dot(
            whole_rows(mixes.at[layer], chunk), wo[layer][...], preferred_element_type=jnp.float32
        )
        for i in range(8):
            head_part[i] = headed[:, i * BLK : (i + 1) * BLK]
        stream[at, :] = stream[at, :] + head_part[tp]
        middle = whole_rows(inputs.at[layer], chunk).astype(jnp.float32) + headed
        post = normalize(middle, gain_after_ref[...].astype(jnp.float32)[layer : layer + 1])
        gate = jnp.dot(post, wg[layer][...], preferred_element_type=jnp.float32)
        up = jnp.dot(post, wu[layer][...], preferred_element_type=jnp.float32)
        hidden = (gate / (1.0 + jnp.exp(-gate)) * up).astype(jnp.bfloat16)
        part = jnp.dot(hidden, wd[layer][...], preferred_element_type=jnp.float32)
        for i in range(8):
            parts[layer, i, at, :] = part[:, i * BLK : (i + 1) * BLK].astype(jnp.bfloat16)
        for d in (1, 3, 2):
            go(sum_send(layer, chunk, d))
        if chunk == 0 and layer + 1 < layers:
            out_cross(layer + 1)

    def sum_send(layer, chunk, d):
        return send(
            parts.at[layer, pl.ds((high + d) % 4 * 2, 2), span(chunk)],
            parts_in.at[layer, d - 1, pl.ds(0, 2), span(chunk)],
            layer,
            RS_Y + 4 * chunk + d,
            at_tp(d),
        )

    def cross_send(layer, chunk):
        return send(
            half_out.at[layer, span(chunk)],
            half_in.at[layer, span(chunk)],
            layer,
            RS_Y + 4 * chunk,
            z_partner,
        )

    def add_up(layer, chunk):
        at = span(chunk)
        for d in (1, 3, 2):
            sum_send(layer, chunk, d).wait_recv()

        def summed(half):
            total = parts[layer, high * 2 + half, at, :].astype(jnp.float32)
            for d in range(3):
                total = total + parts_in[layer, d, half, at, :].astype(jnp.float32)
            return total

        half_out[layer, at, :] = summed(1 - low).astype(jnp.bfloat16)
        go(cross_send(layer, chunk))
        stream[at, :] = stream[at, :] + summed(low)

    def finish(layer, chunk):
        at = span(chunk)
        cross_send(layer, chunk).wait_recv()
        stream[at, :] = stream[at, :] + half_in[layer, at, :].astype(jnp.float32)
        if layer + 1 < layers:
            start_layer(layer + 1, chunk)

    def in_units(stage):
        def run(layer, chunk):
            if chunk % UNIT == UNIT - 1:
                stage(layer, chunk // UNIT)

        return run

    def wavefront(stages):
        for step in range(blocks + LAG * (len(stages) - 1)):
            for i in reversed(range(len(stages))):
                if 0 <= step - LAG * i < blocks:
                    layer, stage = stages[i]
                    stage(layer, step - LAG * i)

    def chain(step):
        return in_units(lambda layer, unit: spread_next(layer, unit, step))

    def front(layer):
        return [
            (layer, pass_layer),
            (layer, project),
            (layer, chain(1)),
            (layer, chain(2)),
            (layer, chain(3)),
            (layer, in_units(spread_back)),
        ]

    def rest(layer):
        return [(layer, attend), (layer, pass_mix), (layer, feed), (layer, add_up), (layer, finish)]

    stream[...] = tokens_ref[...].astype(jnp.float32)
    for chunk in range(blocks):
        start_layer(0, chunk)
    wavefront(front(0))
    for layer in range(layers):
        out_share(layer)
        for unit in range(blocks // UNIT):
            spread_end(layer, unit)
        wavefront(rest(layer) + (front(layer + 1) if layer + 1 < layers else []))
    out_ref[...] = stream[...]
    drain()


def local(
    tokens,
    norm_before,
    query_weight,
    key_weight,
    value_weight,
    output_weight,
    norm_after,
    gate_weight,
    up_weight,
    down_weight,
    block_image,
    image_width,
):
    rows = tokens.shape[0]
    blocks = rows // BLK
    layers = query_weight.shape[0]
    hbm = pl.BlockSpec(memory_space=pl.ANY)
    vmem = pl.BlockSpec(memory_space=pltpu.VMEM)
    smem = pl.BlockSpec(memory_space=pltpu.SMEM)
    bf16, f32 = jnp.bfloat16, jnp.float32
    window, cosine, sine = pl.pallas_call(
        tables_kernel,
        out_shape=(
            jax.ShapeDtypeStruct((blocks, 3), jnp.int32),
            jax.ShapeDtypeStruct((rows, BLK), f32),
            jax.ShapeDtypeStruct((rows, BLK), f32),
        ),
        in_specs=[smem, vmem, smem, vmem],
        out_specs=(smem, vmem, vmem),
        name="tables",
    )(block_image, block_image[None, :], image_width, frequencies())
    return pl.pallas_call(
        functools.partial(layers_kernel, layers),
        out_shape=jax.ShapeDtypeStruct(tokens.shape, f32),
        in_specs=[smem] + [vmem] * 5 + [hbm] * 7,
        out_specs=vmem,
        scratch_shapes=[
            [pltpu.VMEM(query_weight.shape[1:], bf16)] * layers,
            [pltpu.VMEM(key_weight.shape[1:], bf16)] * layers,
            [pltpu.VMEM(value_weight.shape[1:], bf16)] * layers,
            [pltpu.VMEM((8 * BLK, 8 * BLK), bf16)] * layers,
            [pltpu.VMEM(gate_weight.shape[1:], bf16)] * layers,
            [pltpu.VMEM(up_weight.shape[1:], bf16)] * layers,
            [pltpu.VMEM(down_weight.shape[1:], bf16)] * layers,
            pltpu.VMEM((layers, 8, rows, BLK), bf16),
            pltpu.VMEM((layers, 8, rows, BLK), bf16),
            pltpu.VMEM((24 * blocks, BLK, 2 * BLK), bf16),
            pltpu.VMEM((24 * blocks, BLK, 2 * BLK), bf16),
            pltpu.VMEM((rows, BLK), bf16),
            pltpu.VMEM((2 * BLK, WINDOW * BLK), f32),
            pltpu.VMEM((8, BLK, BLK), f32),
            pltpu.VMEM((layers, 8, rows, BLK), bf16),
            pltpu.VMEM((layers, 3, 2, rows, BLK), bf16),
            pltpu.VMEM((layers, rows, BLK), bf16),
            pltpu.VMEM((layers, rows, BLK), bf16),
            pltpu.VMEM((rows, BLK), f32),
            pltpu.SemaphoreType.DMA((7, layers)),
            pltpu.SemaphoreType.DMA((layers, SEMS)),
            pltpu.SemaphoreType.DMA((layers, SEMS)),
        ],
        compiler_params=pltpu.CompilerParams(
            collective_id=0, has_side_effects=True, vmem_limit_bytes=56 << 20
        ),
        name="encoder_layers",
    )(
        window,
        tokens,
        cosine,
        sine,
        norm_before,
        norm_after,
        query_weight,
        key_weight,
        value_weight,
        output_weight,
        gate_weight,
        up_weight,
        down_weight,
    )


def solution(mesh):
    placed = (
        P(("row", "col"), "tp"),
        P(),
        P(None, None, "tp"),
        P(None, None, "tp"),
        P(None, None, "tp"),
        P(None, "tp", None),
        P(),
        P(None, None, "tp"),
        P(None, None, "tp"),
        P(None, "tp", None),
        P(),
        P(),
    )
    return jax.shard_map(
        local, mesh=mesh, in_specs=placed, out_specs=P(("row", "col"), "tp"), check_vma=False
    )
```

```python
import functools

import jax
import jax.numpy as jnp
import numpy as np
from jax import lax
from jax.experimental import pallas as pl
from jax.experimental.pallas import tpu as pltpu
from jax.sharding import PartitionSpec as P

HEAD_DIM = 64
BLK = 128
WINDOW = 30
CHUNK = 256

epsilon = 1e-05
theta = 10000.0
masked = -1e30
MESH = pl.DeviceIdType.MESH

FAR, NEAR, HOP = 3, 3, 3
UNIT = 2

AG_X, AG_A, RS_Y, OUT_W, KV = 0, 32, 64, 80, 96
KV_UP, KV_DOWN, KV_FULL, KV_PART, KV_CORE, KV_BACK, KV_SEMS = 0, 4, 8, 12, 16, 20, 24
SEMS = KV + 4 // UNIT * KV_SEMS


def frequencies():
    half = HEAD_DIM // 2
    each = theta ** (-2.0 * np.arange(half, dtype=np.float64) / HEAD_DIM)
    return np.tile(np.concatenate([each[0::2], each[1::2]]), 4)[None, :].astype(np.float32)


def normalize(values, gain):
    scale = lax.rsqrt(jnp.mean(values * values, axis=-1, keepdims=True) + epsilon)
    return (values * scale * gain).astype(jnp.bfloat16)


def rotate(heads, cosine, sine):
    lane = lax.broadcasted_iota(jnp.int32, heads.shape, 1)
    front = lax.rem(lane, HEAD_DIM) < HEAD_DIM // 2
    width = heads.shape[1]
    other = jnp.where(
        front,
        pltpu.roll(heads, width - HEAD_DIM // 2, 1),
        pltpu.roll(heads, HEAD_DIM // 2, 1),
    )
    return heads * cosine + other * sine


def tables_kernel(image_ref, images_ref, width_ref, frequency_ref, window_ref, cosines, sines):
    blocks = window_ref.shape[0]
    row, col = lax.axis_index("row"), lax.axis_index("col")
    first_block = (row * 4 + col) * blocks
    own_images = [image_ref[first_block + block] for block in range(blocks)]

    images = images_ref[...]
    lane = lax.broadcasted_iota(jnp.int32, (BLK, BLK), 1)
    by_row = lax.rem(lane, HEAD_DIM // 2) < HEAD_DIM // 4
    for block in range(blocks):
        own = own_images[block]
        count = jnp.sum(jnp.where(images == own, 1, 0))
        first = jnp.sum(jnp.where(images < own, 1, 0))
        width = width_ref[own_images[block]]
        begin = jnp.clip(first, first_block - 7 * blocks, first_block + 8 * blocks - WINDOW)
        window_ref[block, 0] = begin - (row // 2 - 1) * 8 * blocks
        window_ref[block, 1] = (begin - first) * BLK
        window_ref[block, 2] = lax.div(count * BLK, width) * width
        slot = (
            lax.broadcasted_iota(jnp.int32, (BLK, BLK), 0) + (first_block + block - first) * BLK
        ).astype(jnp.float32)
        wide = jnp.full((BLK, BLK), width, jnp.int32).astype(jnp.float32)
        patch_row = jnp.floor((slot + 0.5) / wide)
        angle = jnp.where(by_row, patch_row, slot - patch_row * wide) * frequency_ref[...]
        cosine, sine = jnp.cos(angle), jnp.sin(angle)
        cosines[block * BLK : (block + 1) * BLK, :] = cosine
        sines[block * BLK : (block + 1) * BLK, :] = jnp.where(
            lax.rem(lane, HEAD_DIM) < HEAD_DIM // 2, -sine, sine
        )


def layers_kernel(
    layers,
    window_ref,
    tokens_ref,
    cosines,
    sines,
    gain_before_ref,
    gain_after_ref,
    wq_hbm,
    wk_hbm,
    wv_hbm,
    wo_hbm,
    wg_hbm,
    wu_hbm,
    wd_hbm,
    out_ref,
    wq,
    wk,
    wv,
    wo,
    wg,
    wu,
    wd,
    inputs,
    mixes,
    kv_first,
    kv_second,
    query,
    scores,
    head_part,
    parts,
    parts_in,
    half_out,
    half_in,
    stream,
    stream_other,
    weight_sem,
    send_sem,
    recv_sem,
):
    rows = tokens_ref.shape[0]
    blocks = rows // BLK
    row, col, tp = lax.axis_index("row"), lax.axis_index("col"), lax.axis_index("tp")
    high, low = tp // 2, tp % 2
    chip, core = row // 2, row % 2
    other = high * 2 + 1 - low

    def at_tp(step):
        return (row, col, (high + step) % 4 * 2 + low)

    z_partner = (row, col, other)
    core_partner = (chip * 2 + 1 - core, col, tp)
    x_full = ((row + 6 + 4 * core) % 8, col, tp)
    x_part = ((row + 2 + 4 * core) % 8, col, tp)
    z_up = (row, (col + 1) % 4, tp)
    z_down = (row, (col + 3) % 4, tp)

    def weight(number, layer, src, dst):
        return pltpu.make_async_copy(src.at[layer], dst, weight_sem.at[number, layer])

    own_out_rows = pl.ds(pl.multiple_of(tp * BLK, BLK), BLK)

    def weights_in(layer):
        return [
            weight(i, layer, src, dst[layer])
            for i, (src, dst) in enumerate([(wk_hbm, wk), (wv_hbm, wv), (wq_hbm, wq)])
        ]

    def weights_out(layer):
        return weight(3, layer, wo_hbm, wo[layer].at[own_out_rows])

    def weights_feed(layer):
        return [
            weight(4 + i, layer, src, dst[layer])
            for i, (src, dst) in enumerate([(wg_hbm, wg), (wu_hbm, wu), (wd_hbm, wd)])
        ]

    for copy in weights_in(0) + [weights_out(0)]:
        copy.start()

    barrier = pltpu.get_barrier_semaphore()
    peers = [at_tp(1), at_tp(2), at_tp(3), z_partner, core_partner, x_full, x_part, z_up, z_down]
    for peer in peers:
        pl.semaphore_signal(barrier, inc=1, device_id=peer, device_id_type=MESH)
    pl.semaphore_wait(barrier, len(peers))

    pending = []

    def send(src, dst, layer, sem, device):
        return pltpu.make_async_remote_copy(
            src_ref=src,
            dst_ref=dst,
            send_sem=send_sem.at[layer, sem],
            recv_sem=recv_sem.at[layer, sem],
            device_id=device,
            device_id_type=MESH,
        )

    def go(copy):
        copy.start()
        pending.append((None, copy))

    marks = {}

    def drain(mark=None):
        done = pending[: marks[mark] if mark else len(pending)]
        for needed, copy in done:
            if needed is None:
                copy.wait_send()
            else:

                @pl.when(needed)
                def _(copy=copy):
                    copy.wait_send()

        del pending[: len(done)]

    def span(chunk):
        return pl.ds(chunk * BLK, BLK)

    def gather_own(held, layer, base, chunk):
        piece = held.at[tp, span(chunk)]
        go(send(piece, piece, layer, base + 8 * chunk, z_partner))
        for d in (1, 3, 2):
            go(send(piece, piece, layer, base + 8 * chunk + d, at_tp(d)))

    def gather_pass(held, layer, base, chunk):
        piece = held.at[other, span(chunk)]
        send(piece, piece, layer, base + 8 * chunk, z_partner).wait_recv()
        for d in (1, 3, 2):
            go(send(piece, piece, layer, base + 8 * chunk + 3 + d, at_tp(d)))

    def gather_end(held, layer, base, chunk):
        piece = held.at[tp, span(chunk)]
        for d in (1, 3, 2):
            send(piece, piece, layer, base + 8 * chunk + d, at_tp(d)).wait_recv()
        for d in (1, 3, 2):
            send(piece, piece, layer, base + 8 * chunk + 3 + d, at_tp(d)).wait_recv()

    def whole_rows(held, chunk):
        return jnp.concatenate([held[i, span(chunk), :] for i in range(8)], axis=1)

    def out_half(layer, number):
        return wo[layer].at[pl.ds(pl.multiple_of(number * BLK + core * (BLK // 2), 64), BLK // 2)]

    def out_cross(layer):
        weights_out(layer).wait()
        go(send(out_half(layer, tp), out_half(layer, tp), layer, OUT_W, z_partner))

    def out_own(layer):
        for d in (1, 3, 2):
            go(send(out_half(layer, tp), out_half(layer, tp), layer, OUT_W + d, at_tp(d)))

    def out_core(layer, number, sem):
        go(send(out_half(layer, number), out_half(layer, number), layer, OUT_W + 8 + sem, core_partner))

    def out_pass(layer):
        send(out_half(layer, tp), out_half(layer, tp), layer, OUT_W, z_partner).wait_recv()
        for d in (1, 3, 2):
            go(send(out_half(layer, other), out_half(layer, other), layer, OUT_W + 3 + d, at_tp(d)))
        out_core(layer, other, 0)

    def out_share(layer):
        for d in (1, 3, 2):
            held = out_half(layer, tp)
            send(held, held, layer, OUT_W + d, at_tp(d)).wait_recv()
            out_core(layer, (high + 4 - d) % 4 * 2 + low, d)
            send(held, held, layer, OUT_W + 3 + d, at_tp(d)).wait_recv()
            out_core(layer, (high + 4 - d) % 4 * 2 + 1 - low, 3 + d)

    def out_end(layer):
        held = out_half(layer, tp)
        for i in range(7):
            send(held, held, layer, OUT_W + 8 + i, core_partner).wait_recv()

    def start_layer(layer, chunk):
        held = inputs.at[layer]
        held[tp, span(chunk), :] = stream[span(chunk), :].astype(jnp.bfloat16)
        if layer == 0:
            gather_own(held, layer, AG_X, chunk)
        else:
            held[other, span(chunk), :] = stream_other[span(chunk), :].astype(jnp.bfloat16)
            for slot, sem in ((tp, 0), (other, 3)):
                piece = held.at[slot, span(chunk)]
                for d in (1, 3, 2):
                    go(send(piece, piece, layer, AG_X + 8 * chunk + sem + d, at_tp(d)))

    def pass_layer(layer, chunk):
        gather_pass(inputs.at[layer], layer, AG_X, chunk)

    def project(layer, chunk):
        if layer > 0 and chunk == 0:
            marks["layer"] = len(pending)
        gather_end(inputs.at[layer], layer, AG_X, chunk)
        if chunk == 0:
            for copy in weights_in(layer):
                copy.wait()
        held_kv = (kv_first, kv_second)[layer]
        at = span(chunk)
        normed = normalize(
            whole_rows(inputs.at[layer], chunk).astype(jnp.float32),
            gain_before_ref[...].astype(jnp.float32)[layer : layer + 1],
        )
        cosine, sine = cosines[at, :], sines[at, :]
        here = (8 + core * 4 + col) * blocks + chunk
        held_kv[here, :, 0:BLK] = rotate(
            jnp.dot(normed, wk[layer][...], preferred_element_type=jnp.float32), cosine, sine
        ).astype(jnp.bfloat16)
        held_kv[here, :, BLK : 2 * BLK] = jnp.dot(
            normed, wv[layer][...], preferred_element_type=jnp.float32
        ).astype(jnp.bfloat16)
        if chunk % UNIT == UNIT - 1:
            spread_own(layer, chunk // UNIT)
        turned = rotate(
            jnp.dot(normed, wq[layer][...], preferred_element_type=jnp.float32), cosine, sine
        ).astype(jnp.bfloat16)
        query[at, :] = turned * jnp.bfloat16(HEAD_DIM**-0.5)
        if chunk == blocks - 1:
            out_own(layer)
            out_pass(layer)
            if layer == 0:
                for copy in weights_feed(0):
                    copy.start()
                for later in range(1, layers):
                    for copy in weights_in(later) + [weights_out(later)] + weights_feed(later):
                        copy.start()

    def kv_unit(layer, offset, source, unit):
        number = (offset * 8 + core * 4 + source) * blocks + unit * UNIT
        return (kv_first, kv_second)[layer].at[pl.ds(number, UNIT)]

    def kv_send(layer, unit, kind, source, device, slot=None):
        slot = 1 if slot is None else slot
        target = {KV_FULL: 2 - 2 * core, KV_PART: 2 * core}.get(kind, slot)
        return send(
            kv_unit(layer, slot, source, unit),
            kv_unit(layer, target, source, unit),
            layer,
            KV + unit * KV_SEMS + kind + source,
            device,
        )

    def spread_shard(layer, unit, source):
        kv_send(layer, unit, KV_FULL, source, x_full).start()
        kv_send(layer, unit, KV_CORE, source, core_partner).start()
        pending.append((None, kv_send(layer, unit, KV_FULL, source, x_full)))
        pending.append((None, kv_send(layer, unit, KV_CORE, source, core_partner)))

    def spread_own(layer, unit):
        for kind, device, needed in ((KV_UP, z_up, col < 3), (KV_DOWN, z_down, col > 0)):
            copy = kv_send(layer, unit, kind, col, device)

            @pl.when(needed)
            def _(copy=copy):
                copy.start()

            pending.append((needed, copy))
        spread_shard(layer, unit, col)

    def spread_next(layer, unit, step):
        for kind, source, device, here, onward, part in (
            (KV_UP, col - step, z_up, col >= step, col < 3, core == 1),
            (KV_DOWN, col + step, z_down, col + step <= 3, col > 0, core == 0),
        ):
            arrived = kv_send(layer, unit, kind, source, device)
            aside = kv_send(layer, unit, KV_PART, source, x_part)
            full = kv_send(layer, unit, KV_FULL, source, x_full)
            across = kv_send(layer, unit, KV_CORE, source, core_partner)

            @pl.when(here)
            def _(arrived=arrived, aside=aside, full=full, across=across, onward=onward, part=part):
                arrived.wait_recv()

                @pl.when(onward)
                def _():
                    arrived.start()

                full.start()

                @pl.when(part)
                def _():
                    aside.start()

                across.start()

            pending.append((here & onward, arrived))
            pending.append((here & part, aside))
            pending.append((here, full))
            pending.append((here, across))

    def order_of(step):
        return (col + step) % 4

    def spread_back(layer, unit):
        for step in (0, 1, 3, 2):
            source = order_of(step)
            kv_send(layer, unit, KV_FULL, source, x_full).wait_recv()
            go(kv_send(layer, unit, KV_BACK, source, core_partner, slot=2 - 2 * core))

    def spread_end(layer, unit):
        for step in (1, 2, 3):
            source = order_of(step)

            @pl.when(((core == 0) & (source > col)) | ((core == 1) & (source < col)))
            def _(source=source):
                kv_send(layer, unit, KV_PART, source, x_part).wait_recv()

        for source in range(4):
            kv_send(layer, unit, KV_CORE, source, core_partner).wait_recv()
            kv_send(layer, unit, KV_BACK, source, core_partner).wait_recv()

    lane = lax.broadcasted_iota(jnp.int32, (BLK, BLK), 1)
    chunks = WINDOW * BLK // CHUNK
    each = CHUNK // BLK

    def attend(layer, block):
        held_kv = (kv_first, kv_second)[layer]

        def keys_of(begin, chunk, lanes):
            return jnp.concatenate(
                [held_kv[begin + chunk * each + i][:, lanes : lanes + BLK] for i in range(each)], axis=0
            )

        if layer + 1 == layers and block == 0:
            marks["attend"] = len(pending)
        at = span(block)
        begin = window_ref[block, 0]
        shift = window_ref[block, 1]
        filled = window_ref[block, 2]
        turned = query[at, :]
        zero = jnp.zeros_like(turned)
        stacked = jnp.concatenate(
            [jnp.where(lane < HEAD_DIM, turned, zero), jnp.where(lane < HEAD_DIM, zero, turned)],
            axis=0,
        )
        best = jnp.full((2 * BLK, BLK), masked, jnp.float32)
        for chunk in range(chunks):
            found = lax.dot_general(
                stacked,
                keys_of(begin, chunk, 0),
                (((1,), (1,)), ((), ())),
                preferred_element_type=jnp.float32,
            )
            slot = lax.broadcasted_iota(jnp.int32, (1, CHUNK), 1) + (shift + chunk * CHUNK)
            found = jnp.where((slot >= 0) & (slot < filled), found, masked)
            scores[:, chunk * CHUNK : (chunk + 1) * CHUNK] = found
            for part in range(each):
                best = jnp.maximum(best, found[:, part * BLK : (part + 1) * BLK])
        top = jnp.max(best, axis=1, keepdims=True)
        total = jnp.zeros((2 * BLK, BLK), jnp.float32)
        mixed = jnp.zeros((2 * BLK, BLK), jnp.float32)
        for chunk in range(chunks):
            raised = jnp.exp(scores[:, chunk * CHUNK : (chunk + 1) * CHUNK] - top)
            for part in range(each):
                total = total + raised[:, part * BLK : (part + 1) * BLK]
            mixed = mixed + jnp.dot(
                raised.astype(jnp.bfloat16),
                keys_of(begin, chunk, BLK),
                preferred_element_type=jnp.float32,
            )
        mixed = mixed / jnp.sum(total, axis=1, keepdims=True)
        mixes[layer, tp, at, :] = jnp.where(lane < HEAD_DIM, mixed[0:BLK], mixed[BLK:]).astype(
            jnp.bfloat16
        )
        gather_own(mixes.at[layer], layer, AG_A, block)

    def pass_mix(layer, chunk):
        gather_pass(mixes.at[layer], layer, AG_A, chunk)

    def feed(layer, chunk):
        if chunk == 0:
            if layer + 1 == layers:
                drain("attend")
            out_end(layer)
            for copy in weights_feed(layer):
                copy.wait()
        gather_end(mixes.at[layer], layer, AG_A, chunk)
        at = span(chunk)
        headed = jnp.dot(
            whole_rows(mixes.at[layer], chunk), wo[layer][...], preferred_element_type=jnp.float32
        )
        for i in range(8):
            head_part[i] = headed[:, i * BLK : (i + 1) * BLK]
        stream[at, :] = stream[at, :] + head_part[tp]
        if layer + 1 < layers:
            before = inputs[layer, other, at, :].astype(jnp.float32) if layer == 0 else stream_other[at, :]
            stream_other[at, :] = before + head_part[other]
        middle = whole_rows(inputs.at[layer], chunk).astype(jnp.float32) + headed
        post = normalize(middle, gain_after_ref[...].astype(jnp.float32)[layer : layer + 1])
        gate = jnp.dot(post, wg[layer][...], preferred_element_type=jnp.float32)
        up = jnp.dot(post, wu[layer][...], preferred_element_type=jnp.float32)
        hidden = (gate / (1.0 + jnp.exp(-gate)) * up).astype(jnp.bfloat16)
        part = jnp.dot(hidden, wd[layer][...], preferred_element_type=jnp.float32)
        for i in range(8):
            parts[layer, i, at, :] = part[:, i * BLK : (i + 1) * BLK].astype(jnp.bfloat16)
        for d in (1, 3, 2):
            go(sum_send(layer, chunk, d))
        if chunk == 0 and layer + 1 < layers:
            out_cross(layer + 1)

    def sum_send(layer, chunk, d):
        return send(
            parts.at[layer, pl.ds((high + d) % 4 * 2, 2), span(chunk)],
            parts_in.at[layer, d - 1, pl.ds(0, 2), span(chunk)],
            layer,
            RS_Y + 4 * chunk + d,
            at_tp(d),
        )

    def cross_send(layer, chunk):
        halves = pl.ds(0, 2 if layer + 1 < layers else 1)
        return send(
            half_out.at[layer, halves, span(chunk)],
            half_in.at[layer, halves, span(chunk)],
            layer,
            RS_Y + 4 * chunk,
            z_partner,
        )

    def add_up(layer, chunk):
        at = span(chunk)
        for d in (1, 3, 2):
            sum_send(layer, chunk, d).wait_recv()

        def summed(half):
            total = parts[layer, high * 2 + half, at, :].astype(jnp.float32)
            for d in range(3):
                total = total + parts_in[layer, d, half, at, :].astype(jnp.float32)
            return total

        theirs, own = summed(1 - low), summed(low)
        half_out[layer, 0, at, :] = theirs.astype(jnp.bfloat16)
        if layer + 1 < layers:
            half_out[layer, 1, at, :] = own.astype(jnp.bfloat16)
        go(cross_send(layer, chunk))
        stream[at, :] = stream[at, :] + own
        if layer + 1 < layers:
            stream_other[at, :] = stream_other[at, :] + theirs

    def finish(layer, chunk):
        at = span(chunk)
        cross_send(layer, chunk).wait_recv()
        stream[at, :] = stream[at, :] + half_in[layer, 0, at, :].astype(jnp.float32)
        if layer + 1 < layers:
            stream_other[at, :] = stream_other[at, :] + half_in[layer, 1, at, :].astype(jnp.float32)
            start_layer(layer + 1, chunk)

    def in_units(stage):
        def run(layer, chunk):
            if chunk % UNIT == UNIT - 1:
                stage(layer, chunk // UNIT)

        return run

    def wavefront(stages):
        first, offsets = 0, []
        for _, _, lag in stages:
            first += lag if offsets else 0
            offsets.append(first)
        for step in range(blocks + first):
            for (layer, stage, _), offset in reversed(list(zip(stages, offsets))):
                if 0 <= step - offset < blocks:
                    stage(layer, step - offset)

    def chain(step):
        return in_units(lambda layer, unit: spread_next(layer, unit, step))

    def front(layer):
        return ([(layer, pass_layer, FAR)] if layer == 0 else []) + [
            (layer, project, NEAR),
            (layer, chain(1), HOP),
            (layer, chain(2), HOP),
            (layer, chain(3), HOP),
            (layer, in_units(spread_back), HOP),
        ]

    def rest(layer):
        return [
            (layer, attend, 0),
            (layer, pass_mix, FAR),
            (layer, feed, NEAR),
            (layer, add_up, NEAR),
            (layer, finish, FAR),
        ]

    stream[...] = tokens_ref[...].astype(jnp.float32)
    for chunk in range(blocks):
        start_layer(0, chunk)
    out_cross(0)
    wavefront(front(0))
    for layer in range(layers):
        if layer > 0:
            drain("layer")
        out_share(layer)
        for unit in range(blocks // UNIT):
            spread_end(layer, unit)
        wavefront(rest(layer) + (front(layer + 1) if layer + 1 < layers else []))
    out_ref[...] = stream[...]
    drain()


def local(
    tokens,
    norm_before,
    query_weight,
    key_weight,
    value_weight,
    output_weight,
    norm_after,
    gate_weight,
    up_weight,
    down_weight,
    block_image,
    image_width,
):
    rows = tokens.shape[0]
    blocks = rows // BLK
    layers = query_weight.shape[0]
    hbm = pl.BlockSpec(memory_space=pl.ANY)
    vmem = pl.BlockSpec(memory_space=pltpu.VMEM)
    smem = pl.BlockSpec(memory_space=pltpu.SMEM)
    bf16, f32 = jnp.bfloat16, jnp.float32
    window, cosine, sine = pl.pallas_call(
        tables_kernel,
        out_shape=(
            jax.ShapeDtypeStruct((blocks, 3), jnp.int32),
            jax.ShapeDtypeStruct((rows, BLK), f32),
            jax.ShapeDtypeStruct((rows, BLK), f32),
        ),
        in_specs=[smem, vmem, smem, vmem],
        out_specs=(smem, vmem, vmem),
        name="tables",
    )(block_image, block_image[None, :], image_width, frequencies())
    return pl.pallas_call(
        functools.partial(layers_kernel, layers),
        out_shape=jax.ShapeDtypeStruct(tokens.shape, f32),
        in_specs=[smem] + [vmem] * 5 + [hbm] * 7,
        out_specs=vmem,
        scratch_shapes=[
            [pltpu.VMEM(query_weight.shape[1:], bf16)] * layers,
            [pltpu.VMEM(key_weight.shape[1:], bf16)] * layers,
            [pltpu.VMEM(value_weight.shape[1:], bf16)] * layers,
            [pltpu.VMEM((8 * BLK, 8 * BLK), bf16)] * layers,
            [pltpu.VMEM(gate_weight.shape[1:], bf16)] * layers,
            [pltpu.VMEM(up_weight.shape[1:], bf16)] * layers,
            [pltpu.VMEM(down_weight.shape[1:], bf16)] * layers,
            pltpu.VMEM((layers, 8, rows, BLK), bf16),
            pltpu.VMEM((layers, 8, rows, BLK), bf16),
            pltpu.VMEM((24 * blocks, BLK, 2 * BLK), bf16),
            pltpu.VMEM((24 * blocks, BLK, 2 * BLK), bf16),
            pltpu.VMEM((rows, BLK), bf16),
            pltpu.VMEM((2 * BLK, WINDOW * BLK), f32),
            pltpu.VMEM((8, BLK, BLK), f32),
            pltpu.VMEM((layers, 8, rows, BLK), bf16),
            pltpu.VMEM((layers, 3, 2, rows, BLK), bf16),
            pltpu.VMEM((layers, 2, rows, BLK), bf16),
            pltpu.VMEM((layers, 2, rows, BLK), bf16),
            pltpu.VMEM((rows, BLK), f32),
            pltpu.VMEM((rows, BLK), f32),
            pltpu.SemaphoreType.DMA((7, layers)),
            pltpu.SemaphoreType.DMA((layers, SEMS)),
            pltpu.SemaphoreType.DMA((layers, SEMS)),
        ],
        compiler_params=pltpu.CompilerParams(
            collective_id=0, has_side_effects=True, vmem_limit_bytes=56 << 20
        ),
        name="encoder_layers",
    )(
        window,
        tokens,
        cosine,
        sine,
        norm_before,
        norm_after,
        query_weight,
        key_weight,
        value_weight,
        output_weight,
        gate_weight,
        up_weight,
        down_weight,
    )


def solution(mesh):
    placed = (
        P(("row", "col"), "tp"),
        P(),
        P(None, None, "tp"),
        P(None, None, "tp"),
        P(None, None, "tp"),
        P(None, "tp", None),
        P(),
        P(None, None, "tp"),
        P(None, None, "tp"),
        P(None, "tp", None),
        P(),
        P(),
    )
    return jax.shard_map(
        local, mesh=mesh, in_specs=placed, out_specs=P(("row", "col"), "tp"), check_vma=False
    )
```

```python
import functools

import jax
import jax.numpy as jnp
import numpy as np
from jax import lax
from jax.experimental import pallas as pl
from jax.experimental.pallas import tpu as pltpu
from jax.sharding import PartitionSpec as P

HEAD_DIM = 64
BLK = 128
WINDOW = 30
CHUNK = 256

epsilon = 1e-05
theta = 10000.0
masked = -1e30
MESH = pl.DeviceIdType.MESH

FAR, NEAR, HOP = 3, 3, 3
UNIT = 1

AG_X, AG_A, RS_Y, OUT_W, KV = 0, 32, 64, 80, 96
KV_UP, KV_DOWN, KV_FULL, KV_PART, KV_CORE, KV_BACK, KV_SEMS = 0, 4, 8, 12, 16, 20, 24
SEMS = KV + 4 // UNIT * KV_SEMS


def frequencies():
    half = HEAD_DIM // 2
    each = theta ** (-2.0 * np.arange(half, dtype=np.float64) / HEAD_DIM)
    return np.tile(np.concatenate([each[0::2], each[1::2]]), 4)[None, :].astype(np.float32)


def normalize(values, gain):
    scale = lax.rsqrt(jnp.mean(values * values, axis=-1, keepdims=True) + epsilon)
    return (values * scale * gain).astype(jnp.bfloat16)


def rotate(heads, cosine, sine):
    lane = lax.broadcasted_iota(jnp.int32, heads.shape, 1)
    front = lax.rem(lane, HEAD_DIM) < HEAD_DIM // 2
    width = heads.shape[1]
    other = jnp.where(
        front,
        pltpu.roll(heads, width - HEAD_DIM // 2, 1),
        pltpu.roll(heads, HEAD_DIM // 2, 1),
    )
    return heads * cosine + other * sine


def tables_kernel(image_ref, images_ref, width_ref, frequency_ref, window_ref, cosines, sines):
    blocks = window_ref.shape[0]
    row, col = lax.axis_index("row"), lax.axis_index("col")
    first_block = (row * 4 + col) * blocks
    own_images = [image_ref[first_block + block] for block in range(blocks)]

    images = images_ref[...]
    lane = lax.broadcasted_iota(jnp.int32, (BLK, BLK), 1)
    by_row = lax.rem(lane, HEAD_DIM // 2) < HEAD_DIM // 4
    for block in range(blocks):
        own = own_images[block]
        count = jnp.sum(jnp.where(images == own, 1, 0))
        first = jnp.sum(jnp.where(images < own, 1, 0))
        width = width_ref[own_images[block]]
        begin = jnp.clip(first, first_block - 7 * blocks, first_block + 8 * blocks - WINDOW)
        window_ref[block, 0] = begin - (row // 2 - 1) * 8 * blocks
        window_ref[block, 1] = (begin - first) * BLK
        window_ref[block, 2] = lax.div(count * BLK, width) * width
        slot = (
            lax.broadcasted_iota(jnp.int32, (BLK, BLK), 0) + (first_block + block - first) * BLK
        ).astype(jnp.float32)
        wide = jnp.full((BLK, BLK), width, jnp.int32).astype(jnp.float32)
        patch_row = jnp.floor((slot + 0.5) / wide)
        angle = jnp.where(by_row, patch_row, slot - patch_row * wide) * frequency_ref[...]
        cosine, sine = jnp.cos(angle), jnp.sin(angle)
        cosines[block * BLK : (block + 1) * BLK, :] = cosine
        sines[block * BLK : (block + 1) * BLK, :] = jnp.where(
            lax.rem(lane, HEAD_DIM) < HEAD_DIM // 2, -sine, sine
        )


def layers_kernel(
    layers,
    window_ref,
    tokens_ref,
    cosines,
    sines,
    gain_before_ref,
    gain_after_ref,
    wq_hbm,
    wk_hbm,
    wv_hbm,
    wo_hbm,
    wg_hbm,
    wu_hbm,
    wd_hbm,
    out_ref,
    wq,
    wk,
    wv,
    wo,
    wg,
    wu,
    wd,
    inputs,
    mixes,
    kv_first,
    kv_second,
    query,
    scores,
    head_part,
    parts,
    parts_in,
    half_out,
    half_in,
    stream,
    stream_other,
    weight_sem,
    send_sem,
    recv_sem,
):
    rows = tokens_ref.shape[0]
    blocks = rows // BLK
    row, col, tp = lax.axis_index("row"), lax.axis_index("col"), lax.axis_index("tp")
    high, low = tp // 2, tp % 2
    chip, core = row // 2, row % 2
    other = high * 2 + 1 - low

    def at_tp(step):
        return (row, col, (high + step) % 4 * 2 + low)

    z_partner = (row, col, other)
    core_partner = (chip * 2 + 1 - core, col, tp)
    x_full = ((row + 6 + 4 * core) % 8, col, tp)
    x_part = ((row + 2 + 4 * core) % 8, col, tp)
    z_up = (row, (col + 1) % 4, tp)
    z_down = (row, (col + 3) % 4, tp)

    def weight(number, layer, src, dst):
        return pltpu.make_async_copy(src.at[layer], dst, weight_sem.at[number, layer])

    own_out_rows = pl.ds(pl.multiple_of(tp * BLK, BLK), BLK)

    def weights_in(layer):
        return [
            weight(i, layer, src, dst[layer])
            for i, (src, dst) in enumerate([(wk_hbm, wk), (wv_hbm, wv), (wq_hbm, wq)])
        ]

    def weights_out(layer):
        return weight(3, layer, wo_hbm, wo[layer].at[own_out_rows])

    def weights_feed(layer):
        return [
            weight(4 + i, layer, src, dst[layer])
            for i, (src, dst) in enumerate([(wg_hbm, wg), (wu_hbm, wu), (wd_hbm, wd)])
        ]

    for copy in weights_in(0) + [weights_out(0)]:
        copy.start()

    barrier = pltpu.get_barrier_semaphore()
    peers = [at_tp(1), at_tp(2), at_tp(3), z_partner, core_partner, x_full, x_part, z_up, z_down]
    for peer in peers:
        pl.semaphore_signal(barrier, inc=1, device_id=peer, device_id_type=MESH)
    pl.semaphore_wait(barrier, len(peers))

    pending = []

    def send(src, dst, layer, sem, device):
        return pltpu.make_async_remote_copy(
            src_ref=src,
            dst_ref=dst,
            send_sem=send_sem.at[layer, sem],
            recv_sem=recv_sem.at[layer, sem],
            device_id=device,
            device_id_type=MESH,
        )

    def go(copy):
        copy.start()
        pending.append((None, copy))

    marks = {}

    def drain(mark=None):
        done = pending[: marks[mark] if mark else len(pending)]
        for needed, copy in done:
            if needed is None:
                copy.wait_send()
            else:

                @pl.when(needed)
                def _(copy=copy):
                    copy.wait_send()

        del pending[: len(done)]

    def span(chunk):
        return pl.ds(chunk * BLK, BLK)

    def gather_own(held, layer, base, chunk):
        piece = held.at[tp, span(chunk)]
        go(send(piece, piece, layer, base + 8 * chunk, z_partner))
        for d in (1, 3, 2):
            go(send(piece, piece, layer, base + 8 * chunk + d, at_tp(d)))

    def gather_pass(held, layer, base, chunk):
        piece = held.at[other, span(chunk)]
        send(piece, piece, layer, base + 8 * chunk, z_partner).wait_recv()
        for d in (1, 3, 2):
            go(send(piece, piece, layer, base + 8 * chunk + 3 + d, at_tp(d)))

    def gather_end(held, layer, base, chunk):
        piece = held.at[tp, span(chunk)]
        for d in (1, 3, 2):
            send(piece, piece, layer, base + 8 * chunk + d, at_tp(d)).wait_recv()
        for d in (1, 3, 2):
            send(piece, piece, layer, base + 8 * chunk + 3 + d, at_tp(d)).wait_recv()

    def whole_rows(held, chunk):
        return jnp.concatenate([held[i, span(chunk), :] for i in range(8)], axis=1)

    def out_half(layer, number):
        return wo[layer].at[pl.ds(pl.multiple_of(number * BLK + core * (BLK // 2), 64), BLK // 2)]

    def out_cross(layer):
        weights_out(layer).wait()
        go(send(out_half(layer, tp), out_half(layer, tp), layer, OUT_W, z_partner))

    def out_own(layer):
        for d in (1, 3, 2):
            go(send(out_half(layer, tp), out_half(layer, tp), layer, OUT_W + d, at_tp(d)))

    def out_core(layer, number, sem):
        go(send(out_half(layer, number), out_half(layer, number), layer, OUT_W + 8 + sem, core_partner))

    def out_pass(layer):
        send(out_half(layer, tp), out_half(layer, tp), layer, OUT_W, z_partner).wait_recv()
        for d in (1, 3, 2):
            go(send(out_half(layer, other), out_half(layer, other), layer, OUT_W + 3 + d, at_tp(d)))
        out_core(layer, other, 0)

    def out_share(layer):
        for d in (1, 3, 2):
            held = out_half(layer, tp)
            send(held, held, layer, OUT_W + d, at_tp(d)).wait_recv()
            out_core(layer, (high + 4 - d) % 4 * 2 + low, d)
            send(held, held, layer, OUT_W + 3 + d, at_tp(d)).wait_recv()
            out_core(layer, (high + 4 - d) % 4 * 2 + 1 - low, 3 + d)

    def out_end(layer):
        held = out_half(layer, tp)
        for i in range(7):
            send(held, held, layer, OUT_W + 8 + i, core_partner).wait_recv()

    def start_layer(layer, chunk):
        held = inputs.at[layer]
        held[tp, span(chunk), :] = stream[span(chunk), :].astype(jnp.bfloat16)
        if layer == 0:
            gather_own(held, layer, AG_X, chunk)
        else:
            held[other, span(chunk), :] = stream_other[span(chunk), :].astype(jnp.bfloat16)
            for slot, sem in ((tp, 0), (other, 3)):
                piece = held.at[slot, span(chunk)]
                for d in (1, 3, 2):
                    go(send(piece, piece, layer, AG_X + 8 * chunk + sem + d, at_tp(d)))

    def pass_layer(layer, chunk):
        gather_pass(inputs.at[layer], layer, AG_X, chunk)

    def project(layer, chunk):
        if layer > 0 and chunk == 0:
            marks["layer"] = len(pending)
        gather_end(inputs.at[layer], layer, AG_X, chunk)
        if chunk == 0:
            for copy in weights_in(layer):
                copy.wait()
        held_kv = (kv_first, kv_second)[layer]
        at = span(chunk)
        normed = normalize(
            whole_rows(inputs.at[layer], chunk).astype(jnp.float32),
            gain_before_ref[...].astype(jnp.float32)[layer : layer + 1],
        )
        cosine, sine = cosines[at, :], sines[at, :]
        here = (8 + core * 4 + col) * blocks + chunk
        held_kv[here, :, 0:BLK] = rotate(
            jnp.dot(normed, wk[layer][...], preferred_element_type=jnp.float32), cosine, sine
        ).astype(jnp.bfloat16)
        held_kv[here, :, BLK : 2 * BLK] = jnp.dot(
            normed, wv[layer][...], preferred_element_type=jnp.float32
        ).astype(jnp.bfloat16)
        if chunk % UNIT == UNIT - 1:
            spread_own(layer, chunk // UNIT)
        turned = rotate(
            jnp.dot(normed, wq[layer][...], preferred_element_type=jnp.float32), cosine, sine
        ).astype(jnp.bfloat16)
        query[at, :] = turned * jnp.bfloat16(HEAD_DIM**-0.5)
        if chunk == blocks - 1:
            out_own(layer)
            out_pass(layer)
            if layer == 0:
                for copy in weights_feed(0):
                    copy.start()
                for later in range(1, layers):
                    for copy in weights_in(later) + [weights_out(later)] + weights_feed(later):
                        copy.start()

    def kv_unit(layer, offset, source, unit):
        number = (offset * 8 + core * 4 + source) * blocks + unit * UNIT
        return (kv_first, kv_second)[layer].at[pl.ds(number, UNIT)]

    def kv_send(layer, unit, kind, source, device, slot=None):
        slot = 1 if slot is None else slot
        target = {KV_FULL: 2 - 2 * core, KV_PART: 2 * core}.get(kind, slot)
        return send(
            kv_unit(layer, slot, source, unit),
            kv_unit(layer, target, source, unit),
            layer,
            KV + unit * KV_SEMS + kind + source,
            device,
        )

    def spread_shard(layer, unit, source):
        kv_send(layer, unit, KV_FULL, source, x_full).start()
        kv_send(layer, unit, KV_CORE, source, core_partner).start()
        pending.append((None, kv_send(layer, unit, KV_FULL, source, x_full)))
        pending.append((None, kv_send(layer, unit, KV_CORE, source, core_partner)))

    def spread_own(layer, unit):
        for kind, device, needed in ((KV_UP, z_up, col < 3), (KV_DOWN, z_down, col > 0)):
            copy = kv_send(layer, unit, kind, col, device)

            @pl.when(needed)
            def _(copy=copy):
                copy.start()

            pending.append((needed, copy))
        spread_shard(layer, unit, col)

    def spread_next(layer, unit, step):
        for kind, source, device, here, onward, part in (
            (KV_UP, col - step, z_up, col >= step, col < 3, core == 1),
            (KV_DOWN, col + step, z_down, col + step <= 3, col > 0, core == 0),
        ):
            arrived = kv_send(layer, unit, kind, source, device)
            aside = kv_send(layer, unit, KV_PART, source, x_part)
            full = kv_send(layer, unit, KV_FULL, source, x_full)
            across = kv_send(layer, unit, KV_CORE, source, core_partner)

            @pl.when(here)
            def _(arrived=arrived, aside=aside, full=full, across=across, onward=onward, part=part):
                arrived.wait_recv()

                @pl.when(onward)
                def _():
                    arrived.start()

                full.start()

                @pl.when(part)
                def _():
                    aside.start()

                across.start()

            pending.append((here & onward, arrived))
            pending.append((here & part, aside))
            pending.append((here, full))
            pending.append((here, across))

    def order_of(step):
        return (col + step) % 4

    def spread_back(layer, unit):
        for step in (0, 1, 3, 2):
            source = order_of(step)
            kv_send(layer, unit, KV_FULL, source, x_full).wait_recv()
            go(kv_send(layer, unit, KV_BACK, source, core_partner, slot=2 - 2 * core))

    def spread_end(layer, unit):
        for step in (1, 2, 3):
            source = order_of(step)

            @pl.when(((core == 0) & (source > col)) | ((core == 1) & (source < col)))
            def _(source=source):
                kv_send(layer, unit, KV_PART, source, x_part).wait_recv()

        for source in range(4):
            kv_send(layer, unit, KV_CORE, source, core_partner).wait_recv()
            kv_send(layer, unit, KV_BACK, source, core_partner).wait_recv()

    lane = lax.broadcasted_iota(jnp.int32, (BLK, BLK), 1)
    chunks = WINDOW * BLK // CHUNK
    each = CHUNK // BLK

    def attend(layer, block):
        held_kv = (kv_first, kv_second)[layer]

        def keys_of(begin, chunk, lanes):
            return jnp.concatenate(
                [held_kv[begin + chunk * each + i][:, lanes : lanes + BLK] for i in range(each)], axis=0
            )

        if layer + 1 == layers and block == 0:
            marks["attend"] = len(pending)
        at = span(block)
        begin = window_ref[block, 0]
        shift = window_ref[block, 1]
        filled = window_ref[block, 2]
        turned = query[at, :]
        zero = jnp.zeros_like(turned)
        stacked = jnp.concatenate(
            [jnp.where(lane < HEAD_DIM, turned, zero), jnp.where(lane < HEAD_DIM, zero, turned)],
            axis=0,
        )
        best = jnp.full((2 * BLK, BLK), masked, jnp.float32)
        for chunk in range(chunks):
            found = lax.dot_general(
                stacked,
                keys_of(begin, chunk, 0),
                (((1,), (1,)), ((), ())),
                preferred_element_type=jnp.float32,
            )
            slot = lax.broadcasted_iota(jnp.int32, (1, CHUNK), 1) + (shift + chunk * CHUNK)
            found = jnp.where((slot >= 0) & (slot < filled), found, masked)
            scores[:, chunk * CHUNK : (chunk + 1) * CHUNK] = found
            for part in range(each):
                best = jnp.maximum(best, found[:, part * BLK : (part + 1) * BLK])
        top = jnp.max(best, axis=1, keepdims=True)
        total = jnp.zeros((2 * BLK, BLK), jnp.float32)
        mixed = jnp.zeros((2 * BLK, BLK), jnp.float32)
        for chunk in range(chunks):
            raised = jnp.exp(scores[:, chunk * CHUNK : (chunk + 1) * CHUNK] - top)
            for part in range(each):
                total = total + raised[:, part * BLK : (part + 1) * BLK]
            mixed = mixed + jnp.dot(
                raised.astype(jnp.bfloat16),
                keys_of(begin, chunk, BLK),
                preferred_element_type=jnp.float32,
            )
        mixed = mixed / jnp.sum(total, axis=1, keepdims=True)
        mixes[layer, tp, at, :] = jnp.where(lane < HEAD_DIM, mixed[0:BLK], mixed[BLK:]).astype(
            jnp.bfloat16
        )
        gather_own(mixes.at[layer], layer, AG_A, block)

    def pass_mix(layer, chunk):
        gather_pass(mixes.at[layer], layer, AG_A, chunk)

    def feed(layer, chunk):
        if chunk == 0:
            if layer + 1 == layers:
                drain("attend")
            out_end(layer)
            for copy in weights_feed(layer):
                copy.wait()
        gather_end(mixes.at[layer], layer, AG_A, chunk)
        at = span(chunk)
        headed = jnp.dot(
            whole_rows(mixes.at[layer], chunk), wo[layer][...], preferred_element_type=jnp.float32
        )
        for i in range(8):
            head_part[i] = headed[:, i * BLK : (i + 1) * BLK]
        stream[at, :] = stream[at, :] + head_part[tp]
        if layer + 1 < layers:
            before = inputs[layer, other, at, :].astype(jnp.float32) if layer == 0 else stream_other[at, :]
            stream_other[at, :] = before + head_part[other]
        middle = whole_rows(inputs.at[layer], chunk).astype(jnp.float32) + headed
        post = normalize(middle, gain_after_ref[...].astype(jnp.float32)[layer : layer + 1])
        gate = jnp.dot(post, wg[layer][...], preferred_element_type=jnp.float32)
        up = jnp.dot(post, wu[layer][...], preferred_element_type=jnp.float32)
        hidden = (gate / (1.0 + jnp.exp(-gate)) * up).astype(jnp.bfloat16)
        part = jnp.dot(hidden, wd[layer][...], preferred_element_type=jnp.float32)
        for i in range(8):
            parts[layer, i, at, :] = part[:, i * BLK : (i + 1) * BLK].astype(jnp.bfloat16)
        for d in (1, 3, 2):
            go(sum_send(layer, chunk, d))
        if chunk == 0 and layer + 1 < layers:
            out_cross(layer + 1)

    def sum_send(layer, chunk, d):
        return send(
            parts.at[layer, pl.ds((high + d) % 4 * 2, 2), span(chunk)],
            parts_in.at[layer, d - 1, pl.ds(0, 2), span(chunk)],
            layer,
            RS_Y + 4 * chunk + d,
            at_tp(d),
        )

    def cross_send(layer, chunk):
        halves = pl.ds(0, 2 if layer + 1 < layers else 1)
        return send(
            half_out.at[layer, halves, span(chunk)],
            half_in.at[layer, halves, span(chunk)],
            layer,
            RS_Y + 4 * chunk,
            z_partner,
        )

    def add_up(layer, chunk):
        at = span(chunk)
        for d in (1, 3, 2):
            sum_send(layer, chunk, d).wait_recv()

        def summed(half):
            total = parts[layer, high * 2 + half, at, :].astype(jnp.float32)
            for d in range(3):
                total = total + parts_in[layer, d, half, at, :].astype(jnp.float32)
            return total

        theirs, own = summed(1 - low), summed(low)
        half_out[layer, 0, at, :] = theirs.astype(jnp.bfloat16)
        if layer + 1 < layers:
            half_out[layer, 1, at, :] = own.astype(jnp.bfloat16)
        go(cross_send(layer, chunk))
        stream[at, :] = stream[at, :] + own
        if layer + 1 < layers:
            stream_other[at, :] = stream_other[at, :] + theirs

    def finish(layer, chunk):
        at = span(chunk)
        cross_send(layer, chunk).wait_recv()
        stream[at, :] = stream[at, :] + half_in[layer, 0, at, :].astype(jnp.float32)
        if layer + 1 < layers:
            stream_other[at, :] = stream_other[at, :] + half_in[layer, 1, at, :].astype(jnp.float32)
            start_layer(layer + 1, chunk)

    def in_units(stage):
        def run(layer, chunk):
            if chunk % UNIT == UNIT - 1:
                stage(layer, chunk // UNIT)

        return run

    def wavefront(stages):
        first, offsets = 0, []
        for _, _, lag in stages:
            first += lag if offsets else 0
            offsets.append(first)
        for step in range(blocks + first):
            for (layer, stage, _), offset in reversed(list(zip(stages, offsets))):
                if 0 <= step - offset < blocks:
                    stage(layer, step - offset)

    def chain(step):
        return in_units(lambda layer, unit: spread_next(layer, unit, step))

    def front(layer):
        return ([(layer, pass_layer, FAR)] if layer == 0 else []) + [
            (layer, project, NEAR),
            (layer, chain(1), HOP),
            (layer, chain(2), HOP),
            (layer, chain(3), HOP),
            (layer, in_units(spread_back), HOP),
        ]

    def rest(layer):
        return [
            (layer, attend, 0),
            (layer, pass_mix, FAR),
            (layer, feed, NEAR),
            (layer, add_up, NEAR),
            (layer, finish, FAR),
        ]

    stream[...] = tokens_ref[...].astype(jnp.float32)
    for chunk in range(blocks):
        start_layer(0, chunk)
    out_cross(0)
    wavefront(front(0))
    for layer in range(layers):
        if layer > 0:
            drain("layer")
        out_share(layer)
        for unit in range(blocks // UNIT):
            spread_end(layer, unit)
        wavefront(rest(layer) + (front(layer + 1) if layer + 1 < layers else []))
    out_ref[...] = stream[...]
    drain()


def local(
    tokens,
    norm_before,
    query_weight,
    key_weight,
    value_weight,
    output_weight,
    norm_after,
    gate_weight,
    up_weight,
    down_weight,
    block_image,
    image_width,
):
    rows = tokens.shape[0]
    blocks = rows // BLK
    layers = query_weight.shape[0]
    hbm = pl.BlockSpec(memory_space=pl.ANY)
    vmem = pl.BlockSpec(memory_space=pltpu.VMEM)
    smem = pl.BlockSpec(memory_space=pltpu.SMEM)
    bf16, f32 = jnp.bfloat16, jnp.float32
    window, cosine, sine = pl.pallas_call(
        tables_kernel,
        out_shape=(
            jax.ShapeDtypeStruct((blocks, 3), jnp.int32),
            jax.ShapeDtypeStruct((rows, BLK), f32),
            jax.ShapeDtypeStruct((rows, BLK), f32),
        ),
        in_specs=[smem, vmem, smem, vmem],
        out_specs=(smem, vmem, vmem),
        name="tables",
    )(block_image, block_image[None, :], image_width, frequencies())
    return pl.pallas_call(
        functools.partial(layers_kernel, layers),
        out_shape=jax.ShapeDtypeStruct(tokens.shape, f32),
        in_specs=[smem] + [vmem] * 5 + [hbm] * 7,
        out_specs=vmem,
        scratch_shapes=[
            [pltpu.VMEM(query_weight.shape[1:], bf16)] * layers,
            [pltpu.VMEM(key_weight.shape[1:], bf16)] * layers,
            [pltpu.VMEM(value_weight.shape[1:], bf16)] * layers,
            [pltpu.VMEM((8 * BLK, 8 * BLK), bf16)] * layers,
            [pltpu.VMEM(gate_weight.shape[1:], bf16)] * layers,
            [pltpu.VMEM(up_weight.shape[1:], bf16)] * layers,
            [pltpu.VMEM(down_weight.shape[1:], bf16)] * layers,
            pltpu.VMEM((layers, 8, rows, BLK), bf16),
            pltpu.VMEM((layers, 8, rows, BLK), bf16),
            pltpu.VMEM((24 * blocks, BLK, 2 * BLK), bf16),
            pltpu.VMEM((24 * blocks, BLK, 2 * BLK), bf16),
            pltpu.VMEM((rows, BLK), bf16),
            pltpu.VMEM((2 * BLK, WINDOW * BLK), f32),
            pltpu.VMEM((8, BLK, BLK), f32),
            pltpu.VMEM((layers, 8, rows, BLK), bf16),
            pltpu.VMEM((layers, 3, 2, rows, BLK), bf16),
            pltpu.VMEM((layers, 2, rows, BLK), bf16),
            pltpu.VMEM((layers, 2, rows, BLK), bf16),
            pltpu.VMEM((rows, BLK), f32),
            pltpu.VMEM((rows, BLK), f32),
            pltpu.SemaphoreType.DMA((7, layers)),
            pltpu.SemaphoreType.DMA((layers, SEMS)),
            pltpu.SemaphoreType.DMA((layers, SEMS)),
        ],
        compiler_params=pltpu.CompilerParams(
            collective_id=0, has_side_effects=True, vmem_limit_bytes=56 << 20
        ),
        name="encoder_layers",
    )(
        window,
        tokens,
        cosine,
        sine,
        norm_before,
        norm_after,
        query_weight,
        key_weight,
        value_weight,
        output_weight,
        gate_weight,
        up_weight,
        down_weight,
    )


def solution(mesh):
    placed = (
        P(("row", "col"), "tp"),
        P(),
        P(None, None, "tp"),
        P(None, None, "tp"),
        P(None, None, "tp"),
        P(None, "tp", None),
        P(),
        P(None, None, "tp"),
        P(None, None, "tp"),
        P(None, "tp", None),
        P(),
        P(),
    )
    return jax.shard_map(
        local, mesh=mesh, in_specs=placed, out_specs=P(("row", "col"), "tp"), check_vma=False
    )
```
